256 devices in a mesh: seq: 64 (over y, z, core), tp: 4 (over x).
Axes of the slice: x: 4, y: 4, z: 8, core: 2. Of those that a mesh axis runs over, the one named last changes fastest.
Arguments:
- short_hidden: bfloat16 [1024, 1280], P('seq', 'tp'), may hold values from -6 to 6
- long_hidden: bfloat16 [4, 1280], P(None, 'tp'), may hold values from -6 to 6
- short_len: int32 [1024], replicated, may hold values from 1 to 127
- short_slot: int32 [1024], replicated, may hold values from 0 to 2047, as said below
- w_query: bfloat16 [1280, 1280], P(None, 'tp'), may hold values from -0.15625 to 0.15625
- w_key: bfloat16 [1280, 1280], P(None, 'tp'), may hold values from -0.15625 to 0.15625
- w_value: bfloat16 [1280, 1280], P(None, 'tp'), may hold values from -0.15625 to 0.15625
- w_out: bfloat16 [1280, 1280], P('tp'), may hold values from -0.15625 to 0.15625
- qk_gain: float32 [1280], P('tp'), may hold values from 0.7 to 2
- step_rate: float32 [1280], replicated, may hold values from 0.1 to 0.6
- short_keys: bfloat16 [2048, 128, 1280], P('seq', None, 'tp'), may hold values from -0.19921875 to 0.19921875
- short_values: bfloat16 [2048, 128, 1280], P('seq', None, 'tp'), may hold values from -6 to 6
- long_keys: bfloat16 [4, 32768, 1280], P(None, 'seq', 'tp'), may hold values from -0.19921875 to 0.19921875
- long_values: bfloat16 [4, 32768, 1280], P(None, 'seq', 'tp'), may hold values from -6 to 6
Outputs:
- short_out: bfloat16 [1024, 1280], P('seq', 'tp')
- long_out: bfloat16 [4, 1280], P(None, 'tp')
The draws below stay inside these ranges and needn't reach their ends.
Inputs may be any that keep to these rules, and one draw needn't show every extreme that they name: `short_slot`: all slot numbers are distinct; slot s is row s of short_keys and short_values, so it lies on index s // 32 of seq. In every draw some index of seq has all 32 of its slots taken.
All inputs are finite; a program needn't handle non-finite values.
Results may differ from the reference program's by a relative error of at most 0.01.
Values may be sent and summed in bfloat16 or wider, within the bound.
A program may use at most 64 MiB of HBM per device.

```python
import math
import jax
import jax.numpy as jnp
from jax import lax

D = 1280
HEADS = 20
HEAD = 64
CAP = 128
LONG = 4
SLOT_DEV = 32
SHORT = 1024
SLOTS = 2048
LONG_LEN = 32768


def draw_short_slot(key, part):
    base = jax.random.fold_in(key, 11)
    key_hot, key_bias, key_score, key_order = jax.random.split(base, 4)
    shards = SLOTS // SLOT_DEV
    slot_ids = jnp.arange(SLOTS, dtype=jnp.int32)
    shard_of = slot_ids // SLOT_DEV
    hot = jax.random.randint(key_hot, (), 0, shards, dtype=jnp.int32)
    bias = jax.random.randint(key_bias, (shards,), 0, 4, dtype=jnp.int32)
    score = jax.random.randint(key_score, (SLOTS,), 0, 1024, dtype=jnp.int32)
    score = score + bias[shard_of] * 1024
    score = jnp.where(shard_of == hot, score - 8192, score)
    ends = (slot_ids == 0) | (slot_ids == SLOTS - 1)
    score = jnp.where(ends, score - 16384, score) + 16384
    order = jnp.argsort(score * SLOTS + slot_ids, stable=True)
    chosen = order[:SHORT].astype(jnp.int32)
    mixing = jax.random.permutation(key_order, SHORT)
    return chosen[mixing].astype(jnp.int32)


def touch_ends(values, own_key, smallest, top_value):
    shape = values.shape
    spot = [jax.random.randint(jax.random.fold_in(own_key, axis), (), 0, shape[axis]) for axis in range(len(shape))]
    values = values.at[tuple(spot)].set(smallest)
    longest = shape.index(max(shape))
    spot[longest] = (spot[longest] + 1) % shape[longest]
    return values.at[tuple(spot)].set(top_value)


def shard_levels(stream_key, extent, cuts, least, largest):
    def one(dim, blocks):
        steps = jax.random.uniform(jax.random.fold_in(jax.random.fold_in(stream_key, 6), dim), (blocks,), jnp.float32, least / len(cuts), largest / len(cuts))
        return jnp.repeat(jnp.exp(steps), extent[dim] // blocks).reshape((-1,) + (1,) * (len(extent) - dim - 1))

    factor_of = one(*cuts[0])
    for cut in cuts[1:]:
        factor_of = factor_of * one(*cut)
    return factor_of


def scatter_about(key, extent, width, reach, cuts=(), kind=jnp.bfloat16):
    loudness = shard_levels(key, extent, cuts, -0.22, 0.18) if cuts else 1.0
    entries = jax.random.normal(key, extent, jnp.float32) * width * loudness
    return jnp.minimum(jnp.maximum(entries, -reach), reach).astype(kind)


def setup_inputs(seed: int = 0) -> dict:
    splits = jax.random.split(jax.random.key(seed), 15)
    return {
        "short_hidden": scatter_about(splits[0], (SHORT, D), 1.0, 6.0, ((0, 64), (1, 4))),
        "long_hidden": scatter_about(splits[1], (LONG, D), 1.0, 6.0, ((1, 4),)),
        "short_len": touch_ends(jax.random.randint(splits[2], (SHORT,), 1, CAP), jax.random.fold_in(splits[2], 1), 1, CAP - 1).astype(jnp.int32),
        "short_slot": draw_short_slot(jax.random.fold_in(splits[14], 71), 0),
        "w_query": scatter_about(splits[4], (D, D), D ** -0.5, 0.15625, ((1, 4),)),
        "w_key": scatter_about(splits[5], (D, D), D ** -0.5, 0.15625, ((1, 4),)),
        "w_value": scatter_about(splits[6], (D, D), D ** -0.5, 0.15625, ((1, 4),)),
        "w_out": scatter_about(splits[7], (D, D), D ** -0.5, 0.15625, ((0, 4),)),
        "qk_gain": jnp.clip(jnp.exp(math.log(2.0) - 1.0498221 * jax.random.uniform(splits[8], (D,), jnp.float32) ** shard_levels(splits[8], (D,), ((0, 4),), -0.2, 0.2)), 0.7, 2.0),
        "step_rate": jnp.clip(jnp.exp(jax.random.uniform(splits[9], (D,), jnp.float32, math.log(0.1), math.log(0.6))), 0.1, 0.6),
        "short_keys": jnp.clip(jax.random.uniform(splits[10], (SLOTS, CAP, D), jnp.float32, -0.19921875, 0.19921875) * shard_levels(splits[10], (SLOTS, CAP, D), ((0, 64), (2, 4)), -0.4, 0.0), -0.19921875, 0.19921875).astype(jnp.bfloat16),
        "short_values": scatter_about(splits[11], (SLOTS, CAP, D), 1.0, 6.0, ((0, 64), (2, 4))),
        "long_keys": jnp.clip(jax.random.uniform(splits[12], (LONG, LONG_LEN, D), jnp.float32, -0.19921875, 0.19921875) * shard_levels(splits[12], (LONG, LONG_LEN, D), ((1, 64), (2, 4)), -0.4, 0.0), -0.19921875, 0.19921875).astype(jnp.bfloat16),
        "long_values": scatter_about(splits[13], (LONG, LONG_LEN, D), 1.0, 6.0, ((1, 64), (2, 4))),
    }


EPS = 1e-06

def head_unit(x, gain):
    count = x.shape[0]
    parts = x.reshape(count, -1, HEAD)
    parts = parts * lax.rsqrt(lax.optimization_barrier(jnp.sum(parts * parts, -1, keepdims=True)) + EPS)
    return parts.reshape(count, -1) * gain

def row_unit(x):
    return x * lax.rsqrt(lax.optimization_barrier(jnp.mean(x * x, -1, keepdims=True)) + EPS)

def widen(x):
    return lax.optimization_barrier(x.astype(jnp.bfloat16)).astype(jnp.float32)

def cache_terms(query, keys, values, live):
    positions = keys.shape[0]
    key_f = keys.astype(jnp.float32).reshape(positions, HEADS, HEAD)
    value_f = values.astype(jnp.float32).reshape(positions, HEADS, HEAD)
    scores = jnp.einsum('he,phe->hp', query, key_f) * math.sqrt(HEAD)
    weights = jnp.where(live[None, :], jnp.exp(scores), jnp.float32(0.0))
    den = lax.optimization_barrier(jnp.sum(weights, -1))
    num = jnp.einsum('hp,phe->he', widen(weights), value_f)
    return (num, den)

def reference(short_hidden, long_hidden, short_len, short_slot, w_query, w_key, w_value, w_out, qk_gain, step_rate, short_keys, short_values, long_keys, long_values):
    rows = jnp.concatenate([short_hidden, long_hidden], 0)
    count = rows.shape[0]
    q_proj = jnp.dot(rows, w_query, preferred_element_type=jnp.float32)
    k_proj = jnp.dot(rows, w_key, preferred_element_type=jnp.float32)
    v_proj = jnp.dot(rows, w_value, preferred_element_type=jnp.float32)
    query = head_unit(q_proj, qk_gain).astype(jnp.bfloat16)
    new_key = head_unit(k_proj, qk_gain).astype(jnp.bfloat16)
    new_value = v_proj.astype(jnp.bfloat16)
    query_f = query.astype(jnp.float32).reshape(count, HEADS, HEAD)
    key_f = new_key.astype(jnp.float32).reshape(count, HEADS, HEAD)
    value_f = new_value.astype(jnp.float32).reshape(count, HEADS, HEAD)

    def short_one(item):
        query_row, slot, length = item
        keys = lax.dynamic_index_in_dim(short_keys, slot.astype(jnp.int32), 0, keepdims=False)
        values = lax.dynamic_index_in_dim(short_values, slot.astype(jnp.int32), 0, keepdims=False)
        live = jnp.arange(CAP, dtype=jnp.int32) < length
        return cache_terms(query_row, keys, values, live)

    def long_one(item):
        query_row, keys, values = item
        live = jnp.ones((LONG_LEN,), dtype=bool)
        return cache_terms(query_row, keys, values, live)
    short_num, short_den = lax.map(short_one, (query_f[:SHORT], short_slot, short_len))
    long_num, long_den = lax.map(long_one, (query_f[SHORT:], long_keys, long_values))
    cache_num = jnp.concatenate([short_num, long_num], 0)
    cache_den = jnp.concatenate([short_den, long_den], 0)
    own = jnp.exp(lax.optimization_barrier(jnp.sum(query_f * key_f, -1)) * math.sqrt(HEAD))
    den = cache_den + own
    num = cache_num + widen(own)[..., None] * value_f
    attended = (num / den[..., None]).reshape(count, D).astype(jnp.bfloat16)
    proj = jnp.dot(attended, w_out, preferred_element_type=jnp.float32)
    state = rows.astype(jnp.float32)
    update = state + step_rate * (row_unit(proj) - state)
    result = row_unit(update).astype(jnp.bfloat16)
    return (result[:SHORT], result[SHORT:])
```

```python
import functools
import math

import jax
import jax.numpy as jnp
from jax import lax
from jax.experimental import pallas as pl
from jax.experimental.pallas import tpu as pltpu
from jax.sharding import PartitionSpec as P

HEAD = 64
EPS = 1e-06
MESH = pl.DeviceIdType.MESH
F32 = jnp.float32
BF16 = jnp.bfloat16
GRID = {64: (4, 8, 2), 8: (2, 2, 2)}
GROUP = 8
LROWS = 8


def dot(a, b):
    return lax.dot_general(a, b, (((1,), (0,)), ((), ())), preferred_element_type=F32)


def dot_t(a, b):
    return lax.dot_general(a, b, (((1,), (1,)), ((), ())), preferred_element_type=F32)


def lanes(shape):
    return lax.broadcasted_iota(jnp.int32, shape, 1)


def rows_of(shape):
    return lax.broadcasted_iota(jnp.int32, shape, 0)


def head_sums(x):
    head = lanes(x.shape) // HEAD
    return [
        jnp.sum(jnp.where(head == h, x, 0.0), axis=1, keepdims=True)
        for h in range(x.shape[1] // HEAD)
    ]


def spread(columns, shape):
    head = lanes(shape) // HEAD
    out = jnp.broadcast_to(columns[0], shape)
    for h in range(1, len(columns)):
        out = jnp.where(head == h, columns[h], out)
    return out


def head_unit(x, gain):
    scale = [lax.rsqrt(s + EPS) for s in head_sums(x * x)]
    return x * spread(scale, x.shape) * gain


def row_unit(x):
    return x * lax.rsqrt(jnp.sum(x * x, axis=1, keepdims=True) * (1.0 / x.shape[1]) + EPS)


def by_head(q):
    head = lanes(q.shape) // HEAD
    return jnp.concatenate(
        [jnp.where(head == h, q, 0.0) for h in range(q.shape[1] // HEAD)], axis=0
    ).astype(BF16)


def attend(q, keys, values, valid):
    r, width = q.shape
    heads = width // HEAD
    scores = dot(by_head(q), keys)
    weights = jnp.where(jnp.concatenate([valid] * heads, axis=0), jnp.exp(scores), 0.0)
    den = jnp.sum(weights, axis=1, keepdims=True)
    full = dot_t(weights.astype(BF16), values)
    head = lanes((r, width)) // HEAD
    num = full[:r]
    for h in range(1, heads):
        num = jnp.where(head == h, full[h * r : (h + 1) * r], num)
    return num, [den[h * r : (h + 1) * r] for h in range(heads)]


def tail_of(part, columns):
    half = part.shape[1] // 2
    lane = lanes(part.shape)
    out = jnp.where(lane < half, part, 0.0)
    for h, column in enumerate(columns):
        out = jnp.where(lane == half + h, column, out)
    return out


def columns_of(tail, heads):
    half = tail.shape[1] // 2
    lane = lanes(tail.shape)
    return [
        jnp.sum(jnp.where(lane == half + h, tail, 0.0), axis=1, keepdims=True)
        for h in range(heads)
    ]


def side_by_side(ref, lo, hi):
    return jnp.concatenate([ref[i] for i in range(lo, hi)], axis=1)


def far_first(n):
    return sorted(range(1, n), key=lambda d: -min(d, n - d))


def kernel(
    sizes,
    hid_s, hid_l, len_h, slot_h, wq_h, wk_h, wv_h, wo_h, gain_h, rate_h, ks_h, vs_h, kl_h, vl_h,
    out_s, out_l,
    hbuf, hlbuf, len_v, slot_v, wq, wk, wv, wo, gain_v, rate_v, ks, vs, kl, vl,
    sel, sel_t, qz, f2s, f2r, r1s, r1r, r2s, r2r, acc, l1s, l1r, l2s, l2r, x2s, x2r, x3s, x3r,
    lsem, xs_s, xs_r, xl_s, xl_r, f1_s, f1_r, f2_s, f2_rs, l1_s, l1_rs, l2_s, l2_rs,
    r1_s, r1_rs, r2_s, r2_rs, x2_s, x2_rs, x3_s, x3_rs,
):
    ny, nz, nc, nx = sizes
    nw = ny * nc
    ns, width = hid_s.shape
    long_count = hid_l.shape[0]
    depth = wq_h.shape[1]
    heads = width // HEAD
    slot_dev, cap = ks_h.shape[0], ks_h.shape[2]
    total_rows = slot_h.shape[0]
    s = lax.axis_index("seq")
    t = lax.axis_index("tp")
    c = lax.rem(s, nc)
    z = lax.rem(s // nc, nz)
    y = s // (nc * nz)
    w = y * nc + c

    def at(y_, z_, c_, t_):
        return {"seq": (y_ * nz + z_) * nc + c_, "tp": t_}

    x_peer = {d: at(y, z, c, lax.rem(t + d, nx)) for d in far_first(nx)}
    z_peer = {d: at(y, lax.rem(z + d, nz), c, t) for d in far_first(nz)}
    w_at = {d: lax.rem(w + d, nw) for d in far_first(nw)}
    w_peer = {d: at(v // nc, z, lax.rem(v, nc), t) for d, v in w_at.items()}

    barrier = pltpu.get_barrier_semaphore()
    everyone = [*x_peer.values(), *z_peer.values(), *w_peer.values()]
    for peer in everyone:
        pl.semaphore_signal(barrier, inc=1, device_id=peer, device_id_type=MESH)

    local = {}
    for i, (name, src, dst) in enumerate((
        ("hs", hid_s, hbuf.at[t]), ("hl", hid_l, hlbuf.at[t]), ("slot", slot_h, slot_v), ("len", len_h, len_v),
        ("gain", gain_h, gain_v), ("rate", rate_h, rate_v), ("wq", wq_h, wq), ("kl", kl_h, kl), ("vl", vl_h, vl),
        ("wk", wk_h, wk), ("wv", wv_h, wv), ("ks", ks_h, ks), ("vs", vs_h, vs), ("wo", wo_h, wo),
    )):
        local[name] = pltpu.make_async_copy(src, dst, lsem.at[i])
        local[name].start()

    sent = []

    def send(src, dst, s_sem, r_sem, peer):
        copy = pltpu.make_async_remote_copy(
            src_ref=src, dst_ref=dst, send_sem=s_sem, recv_sem=r_sem, device_id=peer, device_id_type=MESH
        )
        copy.start()
        sent.append(copy)
        return copy

    pl.semaphore_wait(barrier, len(everyone))
    x1 = [send(hid_s, hbuf.at[t], xs_s.at[d], xs_r.at[d], p) for d, p in x_peer.items()]
    x1l = [send(hid_l, hlbuf.at[t], xl_s.at[d], xl_r.at[d], p) for d, p in x_peer.items()]

    qz[:, 1 - c] = jnp.zeros((nz, ns, width), BF16)
    local["slot"].wait()
    local["len"].wait()
    span = nz * nc * ns
    per = 128 // (nc * ns)
    ids = rows_of((nw * slot_dev, 128))
    ids = ids // (nc * slot_dev) * (nz * nc * slot_dev) + z * (nc * slot_dev) + lax.rem(ids, nc * slot_dev)
    for i in range(span // 128):
        row = slot_v[pl.ds(y * (span // 128) + i, 1), :]
        hit = jnp.where(ids == row, 1.0, 0.0)
        sel[:, i * 128 : (i + 1) * 128] = hit.astype(BF16)
        sel_t[i * per : (i + 1) * per] = (
            jnp.transpose(hit).astype(BF16).reshape(per, nc, ns, nw * slot_dev)
        )
    mine = rows_of((slot_dev, 128)) + s * slot_dev
    size = jnp.zeros((slot_dev, 128), F32)
    for i in range(total_rows):
        size += jnp.where(mine == slot_v[i : i + 1, :], len_v[i : i + 1, :].astype(F32), 0.0)
    size = jnp.sum(size, axis=1, keepdims=True)

    for name in ("hs", "gain", "wq"):
        local[name].wait()
    for copy in x1:
        copy.wait_recv()
    gain = gain_v[...].reshape(1, width)
    hidden = jnp.concatenate([hbuf[i] for i in range(nx)], axis=1)
    q_short = head_unit(dot_t(hidden, wq[...]), gain).astype(BF16)
    qz[z, c] = q_short
    f1 = [send(qz.at[z, c], qz.at[z, c], f1_s.at[d], f1_r.at[d], p) for d, p in z_peer.items()]

    local["hl"].wait()
    for copy in x1l:
        copy.wait_recv()
    hidden_l = jnp.concatenate([hlbuf[i].astype(F32) for i in range(nx)], axis=1)
    hidden_l = jnp.concatenate([hidden_l, jnp.zeros((LROWS - long_count, depth), F32)], axis=0)
    q_long = head_unit(dot_t(hidden_l.astype(BF16), wq[...]), gain).astype(BF16)
    local["kl"].wait()
    local["vl"].wait()
    positions = kl.shape[0] * kl.shape[2]
    valid = lanes((LROWS, positions)) // kl.shape[2] == rows_of((LROWS, positions))
    num, den = attend(
        q_long.astype(F32) * math.sqrt(HEAD),
        side_by_side(kl, 0, long_count),
        side_by_side(vl, 0, long_count),
        valid,
    )
    l1s[:, :width] = num
    l1s[:, width - 64 :] = tail_of(l1s[:, width - 64 :], den)
    l1r[z] = l1s[...]
    l1 = [send(l1s, l1r.at[z], l1_s.at[d], l1_rs.at[d], p) for d, p in z_peer.items()]

    local["wk"].wait()
    local["wv"].wait()
    state = jnp.concatenate([hidden.astype(F32), hidden_l], axis=0)
    every = state.astype(BF16)
    query = jnp.concatenate([q_short.astype(F32), q_long.astype(F32)], axis=0)
    new_key = head_unit(dot_t(every, wk[...]), gain).astype(BF16).astype(F32)
    new_value = dot_t(every, wv[...]).astype(BF16).astype(F32)
    own = [jnp.exp(v * math.sqrt(HEAD)) for v in head_sums(query * new_key)]
    own_value = spread([v.astype(BF16).astype(F32) for v in own], new_value.shape) * new_value

    for copy in f1:
        copy.wait_recv()
    picked = dot(sel[...], qz[...].reshape(span, width)).astype(BF16)
    f2s[...] = picked.reshape(nw, slot_dev, width)
    f2 = [send(f2s.at[v], f2r.at[w], f2_s.at[d], f2_rs.at[d], w_peer[d]) for d, v in w_at.items()]
    f2r[w] = f2s[w]

    for copy in l1:
        copy.wait_recv()
    l2s[...] = jnp.sum(l1r[...], axis=0)
    l2r[w] = l2s[...]
    l2 = [send(l2s, l2r.at[w], l2_s.at[d], l2_rs.at[d], p) for d, p in w_peer.items()]

    local["ks"].wait()
    local["vs"].wait()
    for copy in f2:
        copy.wait_recv()
    q_slot = jnp.sum(f2r[...].astype(F32), axis=0) * math.sqrt(HEAD)
    reach = GROUP * cap
    place = lanes((GROUP, reach))
    for g in range(slot_dev // GROUP):
        part = slice(g * GROUP, (g + 1) * GROUP)
        inside = place - rows_of((GROUP, reach)) * cap
        valid = jnp.logical_and(inside >= 0, inside < size[part].astype(jnp.int32))
        num, den = attend(
            q_slot[part],
            side_by_side(ks, g * GROUP, (g + 1) * GROUP),
            side_by_side(vs, g * GROUP, (g + 1) * GROUP),
            valid,
        )
        acc[part, :width] = num
        acc[part, width - 64 :] = tail_of(acc[part, width - 64 :], den)
    r1s[...] = acc[...].astype(BF16)
    r1 = [send(r1s, r1r.at[w], r1_s.at[d], r1_rs.at[d], p) for d, p in w_peer.items()]
    r1r[w] = r1s[...]

    local["rate"].wait()
    local["wo"].wait()
    rate = rate_v[...].reshape(1, depth)

    def attended(sums, lo, hi):
        own_part = [v[lo:hi] for v in own]
        under = [a + b for a, b in zip(columns_of(sums[:, width - 64 :], heads), own_part, strict=True)]
        return ((sums[:, :width] + own_value[lo:hi]) / spread(under, (hi - lo, width))).astype(BF16)

    def updated(proj, lo, hi):
        update = state[lo:hi] + rate * (row_unit(proj) - state[lo:hi])
        result = row_unit(update)
        return pltpu.roll(result, lax.rem(depth - t * width, depth), 1)[:, :width]

    for copy in l2:
        copy.wait_recv()
    x3s[...] = dot(attended(jnp.sum(l2r[...], axis=0), ns, ns + LROWS), wo[...])
    x3r[t] = x3s[...]
    x3 = [send(x3s, x3r.at[t], x3_s.at[d], x3_rs.at[d], p) for d, p in x_peer.items()]

    for copy in r1:
        copy.wait_recv()
    back = dot(sel_t[:, c].reshape(nz * ns, nw * slot_dev), r1r[...].reshape(nw * slot_dev, width + 64))
    r2s[...] = back.astype(BF16).reshape(nz, ns, width + 64)
    r2 = [
        send(r2s.at[lax.rem(z + d, nz)], r2r.at[z], r2_s.at[d], r2_rs.at[d], p)
        for d, p in z_peer.items()
    ]
    r2r[z] = r2s[z]

    for copy in x3:
        copy.wait_recv()
    out_l[...] = updated(jnp.sum(x3r[...], axis=0), ns, ns + LROWS)[:long_count].astype(BF16)

    for copy in r2:
        copy.wait_recv()
    sums = jnp.sum(r2r[...].astype(F32), axis=0)
    x2s[...] = dot(attended(sums, 0, ns), wo[...]).astype(BF16)
    x2r[t] = x2s[...]
    x2 = [send(x2s, x2r.at[t], x2_s.at[d], x2_rs.at[d], p) for d, p in x_peer.items()]
    for copy in x2:
        copy.wait_recv()
    out_s[...] = updated(jnp.sum(x2r[...].astype(F32), axis=0), 0, ns).astype(BF16)

    for copy in sent:
        copy.wait_send()


def on_device(
    sizes,
    short_hidden, long_hidden, short_len, short_slot, w_query, w_key, w_value, w_out, qk_gain, step_rate,
    short_keys, short_values, long_keys, long_values,
):
    ny, nz, nc, nx = sizes
    nw = ny * nc
    ns, width = short_hidden.shape
    long_count = long_hidden.shape[0]
    depth = w_query.shape[0]
    slot_dev = short_keys.shape[0]
    wide = width + 64
    total = short_slot.shape[0]
    span = nz * nc * ns
    dma = pltpu.SemaphoreType.DMA
    args = (
        short_hidden, long_hidden, short_len.reshape(total // 128, 128), short_slot.reshape(total // 128, 128),
        w_query.T, w_key.T, w_value.T, w_out, qk_gain, step_rate,
        *(a.transpose(0, 2, 1) for a in (short_keys, short_values, long_keys, long_values)),
    )
    vmem = pltpu.VMEM
    scratch = [
        vmem((nx, ns, width), BF16), vmem((nx, long_count, width), BF16),
        *(vmem(a.shape, a.dtype) for a in args[2:]),
        vmem((nw * slot_dev, span), BF16), vmem((nz, nc, ns, nw * slot_dev), BF16),
        vmem((nz, nc, ns, width), BF16),
        vmem((nw, slot_dev, width), BF16), vmem((nw, slot_dev, width), BF16),
        vmem((slot_dev, wide), BF16), vmem((nw, slot_dev, wide), BF16),
        vmem((nz, ns, wide), BF16), vmem((nz, ns, wide), BF16), vmem((slot_dev, wide), F32),
        vmem((LROWS, wide), F32), vmem((nz, LROWS, wide), F32),
        vmem((LROWS, wide), F32), vmem((nw, LROWS, wide), F32),
        vmem((ns, depth), BF16), vmem((nx, ns, depth), BF16),
        vmem((LROWS, depth), F32), vmem((nx, LROWS, depth), F32),
        dma((14,)), dma((nx,)), dma((nx,)), dma((nx,)), dma((nx,)), dma((nz,)), dma((nz,)), dma((nw,)), dma((nw,)),
        dma((nz,)), dma((nz,)), dma((nw,)), dma((nw,)), dma((nw,)), dma((nw,)), dma((nz,)), dma((nz,)),
        dma((nx,)), dma((nx,)), dma((nx,)), dma((nx,)),
    ]
    return pl.pallas_call(
        functools.partial(kernel, sizes),
        out_shape=(
            jax.ShapeDtypeStruct(short_hidden.shape, BF16),
            jax.ShapeDtypeStruct(long_hidden.shape, BF16),
        ),
        in_specs=[pl.BlockSpec(memory_space=pl.ANY)] * len(args),
        out_specs=(pl.BlockSpec(memory_space=vmem), pl.BlockSpec(memory_space=vmem)),
        scratch_shapes=scratch,
        compiler_params=pltpu.CompilerParams(collective_id=0, has_side_effects=True),
    )(*args)


def solution(mesh):
    sizes = (*GRID[mesh.shape["seq"]], mesh.shape["tp"])
    return jax.shard_map(
        functools.partial(on_device, sizes),
        mesh=mesh,
        in_specs=(
            P("seq", "tp"),
            P(None, "tp"),
            P(),
            P(),
            P(None, "tp"),
            P(None, "tp"),
            P(None, "tp"),
            P("tp", None),
            P("tp"),
            P(),
            P("seq", None, "tp"),
            P("seq", None, "tp"),
            P(None, "seq", "tp"),
            P(None, "seq", "tp"),
        ),
        out_specs=(P("seq", "tp"), P(None, "tp")),
        check_vma=False,
    )
```

```python
import functools
import math

import jax
import jax.numpy as jnp
from jax import lax
from jax.experimental import pallas as pl
from jax.experimental.pallas import tpu as pltpu
from jax.sharding import PartitionSpec as P

HEAD = 64
EPS = 1e-06
MESH = pl.DeviceIdType.MESH
F32 = jnp.float32
BF16 = jnp.bfloat16
GRID = {64: (4, 8, 2), 8: (2, 2, 2)}
GROUP = 8
LROWS = 8


def dot(a, b):
    return lax.dot_general(a, b, (((1,), (0,)), ((), ())), preferred_element_type=F32)


def dot_t(a, b):
    return lax.dot_general(a, b, (((1,), (1,)), ((), ())), preferred_element_type=F32)


def lanes(shape):
    return lax.broadcasted_iota(jnp.int32, shape, 1)


def rows_of(shape):
    return lax.broadcasted_iota(jnp.int32, shape, 0)


def head_sums(x):
    head = lanes(x.shape) // HEAD
    return [
        jnp.sum(jnp.where(head == h, x, 0.0), axis=1, keepdims=True)
        for h in range(x.shape[1] // HEAD)
    ]


def spread(columns, shape):
    head = lanes(shape) // HEAD
    out = jnp.broadcast_to(columns[0], shape)
    for h in range(1, len(columns)):
        out = jnp.where(head == h, columns[h], out)
    return out


def head_unit(x, gain):
    scale = [lax.rsqrt(s + EPS) for s in head_sums(x * x)]
    return x * spread(scale, x.shape) * gain


def row_unit(x):
    return x * lax.rsqrt(jnp.sum(x * x, axis=1, keepdims=True) * (1.0 / x.shape[1]) + EPS)


def by_head(q):
    head = lanes(q.shape) // HEAD
    return jnp.concatenate(
        [jnp.where(head == h, q, 0.0) for h in range(q.shape[1] // HEAD)], axis=0
    ).astype(BF16)


def attend(q, keys, values, valid):
    r, width = q.shape
    heads = width // HEAD
    scores = dot(by_head(q), keys)
    weights = jnp.where(jnp.concatenate([valid] * heads, axis=0), jnp.exp(scores), 0.0)
    den = jnp.sum(weights, axis=1, keepdims=True)
    full = dot_t(weights.astype(BF16), values)
    head = lanes((r, width)) // HEAD
    num = full[:r]
    for h in range(1, heads):
        num = jnp.where(head == h, full[h * r : (h + 1) * r], num)
    return num, [den[h * r : (h + 1) * r] for h in range(heads)]


def tail_of(part, columns):
    half = part.shape[1] // 2
    lane = lanes(part.shape)
    out = jnp.where(lane < half, part, 0.0)
    for h, column in enumerate(columns):
        out = jnp.where(lane == half + h, column, out)
    return out


def columns_of(tail, heads):
    half = tail.shape[1] // 2
    lane = lanes(tail.shape)
    return [
        jnp.sum(jnp.where(lane == half + h, tail, 0.0), axis=1, keepdims=True)
        for h in range(heads)
    ]


def side_by_side(ref, lo, hi):
    return jnp.concatenate([ref[i] for i in range(lo, hi)], axis=1)


def far_first(n):
    return sorted(range(1, n), key=lambda d: -min(d, n - d))


def kernel(
    sizes,
    hid_s, hid_l, len_h, slot_h, wq_h, wk_h, wv_h, wo_h, gain_h, rate_h, ks_h, vs_h, kl_h, vl_h,
    out_s, out_l,
    hbuf, hlbuf, index_v, wq, wkv, wo, gain_v, rate_v, cache_v, long_v,
    sel, sel_t, qz, f2s, f2r, r1s, r1r, r2s, r2r, acc, l1s, l1r, l2s, l2r, x2s, x2r, x3s, x3r,
    local_sem, send_sem, recv_sem,
):
    ny, nz, nc, nx = sizes
    nw = ny * nc
    ns, width = hid_s.shape
    long_count = hid_l.shape[0]
    depth = wq_h.shape[1]
    heads = width // HEAD
    slot_dev, cap = ks_h.shape[0], ks_h.shape[2]
    total_rows = slot_h.shape[0]
    s = lax.axis_index("seq")
    t = lax.axis_index("tp")
    c = lax.rem(s, nc)
    z = lax.rem(s // nc, nz)
    y = s // (nc * nz)
    w = y * nc + c

    def at(y_, z_, c_, t_):
        return {"seq": (y_ * nz + z_) * nc + c_, "tp": t_}

    x_peer = {d: at(y, z, c, lax.rem(t + d, nx)) for d in far_first(nx)}
    z_peer = {d: at(y, lax.rem(z + d, nz), c, t) for d in far_first(nz)}
    w_at = {d: lax.rem(w + d, nw) for d in far_first(nw)}
    w_peer = {d: at(v // nc, z, lax.rem(v, nc), t) for d, v in w_at.items()}

    barrier = pltpu.get_barrier_semaphore()
    everyone = [*x_peer.values(), *z_peer.values(), *w_peer.values()]
    for peer in everyone:
        pl.semaphore_signal(barrier, inc=1, device_id=peer, device_id_type=MESH)

    local = {}
    for i, (name, dst, *srcs) in enumerate((
        ("hs", hbuf.at[t], hid_s), ("index", index_v, slot_h, len_h), ("gain", gain_v, gain_h), ("wq", wq, wq_h),
        ("hl", hlbuf.at[t], hid_l), ("long", long_v, kl_h, vl_h), ("wkv", wkv, wk_h, wv_h), ("cache", cache_v, ks_h, vs_h),
        ("wo", wo, wo_h), ("rate", rate_v, rate_h),
    )):
        for k, src in enumerate(srcs):
            pltpu.make_async_copy(src, dst.at[k] if len(srcs) > 1 else dst, local_sem.at[i]).start()
        local[name] = pltpu.make_async_copy(dst, dst, local_sem.at[i])
    kl, vl = long_v.at[0], long_v.at[1]
    ks, vs = cache_v.at[0], cache_v.at[1]
    slot_v, len_v = index_v.at[0], index_v.at[1]

    sent = []

    def stage(blocks, copies):
        k = len(sent)
        for src, dst, peer in copies:
            pltpu.make_async_remote_copy(
                src_ref=src, dst_ref=dst, send_sem=send_sem.at[k], recv_sem=recv_sem.at[k],
                device_id=peer, device_id_type=MESH,
            ).start()
        sent.append(pltpu.make_async_copy(blocks, blocks, send_sem.at[k]))
        return pltpu.make_async_copy(blocks, blocks, recv_sem.at[k])

    pl.semaphore_wait(barrier, len(everyone))
    x1 = stage(hbuf.at[: nx - 1], [(hid_s, hbuf.at[t], p) for p in x_peer.values()])
    x1l = stage(hlbuf.at[: nx - 1], [(hid_l, hlbuf.at[t], p) for p in x_peer.values()])

    qz[:, 1 - c] = jnp.zeros((nz, ns, width), BF16)
    local["index"].wait()
    span = nz * nc * ns
    per = 128 // (nc * ns)
    ids = rows_of((nw * slot_dev, 128))
    ids = ids // (nc * slot_dev) * (nz * nc * slot_dev) + z * (nc * slot_dev) + lax.rem(ids, nc * slot_dev)
    for i in range(span // 128):
        row = slot_v[pl.ds(y * (span // 128) + i, 1), :]
        hit = jnp.where(ids == row, 1.0, 0.0)
        sel[:, i * 128 : (i + 1) * 128] = hit.astype(BF16)
        sel_t[i * per : (i + 1) * per] = (
            jnp.transpose(hit).astype(BF16).reshape(per, nc, ns, nw * slot_dev)
        )
    mine = rows_of((slot_dev, 128)) + s * slot_dev
    size = jnp.zeros((slot_dev, 128), F32)
    for i in range(total_rows):
        size += jnp.where(mine == slot_v[i : i + 1, :], len_v[i : i + 1, :].astype(F32), 0.0)
    size = jnp.sum(size, axis=1, keepdims=True)

    for name in ("hs", "gain", "wq"):
        local[name].wait()
    x1.wait()
    gain = gain_v[...].reshape(1, width)
    hidden = jnp.concatenate([hbuf[i] for i in range(nx)], axis=1)
    q_short = head_unit(dot_t(hidden, wq[...]), gain).astype(BF16)
    qz[z, c] = q_short
    f1 = stage(qz.at[: nz - 1, c], [(qz.at[z, c], qz.at[z, c], p) for p in z_peer.values()])

    local["hl"].wait()
    x1l.wait()
    hidden_l = jnp.concatenate([hlbuf[i].astype(F32) for i in range(nx)], axis=1)
    hidden_l = jnp.concatenate([hidden_l, jnp.zeros((LROWS - long_count, depth), F32)], axis=0)
    q_long = head_unit(dot_t(hidden_l.astype(BF16), wq[...]), gain).astype(BF16)
    local["long"].wait()
    positions = kl.shape[0] * kl.shape[2]
    valid = lanes((LROWS, positions)) // kl.shape[2] == rows_of((LROWS, positions))
    num, den = attend(
        q_long.astype(F32) * math.sqrt(HEAD),
        side_by_side(kl, 0, long_count),
        side_by_side(vl, 0, long_count),
        valid,
    )
    l1s[:, :width] = num
    l1s[:, width - 64 :] = tail_of(l1s[:, width - 64 :], den)
    l1r[w] = l1s[...]
    l1 = stage(l1r.at[: nw - 1], [(l1s, l1r.at[w], p) for p in w_peer.values()])

    local["wkv"].wait()
    state = jnp.concatenate([hidden.astype(F32), hidden_l], axis=0)
    every = state.astype(BF16)
    query = jnp.concatenate([q_short.astype(F32), q_long.astype(F32)], axis=0)
    new_key = head_unit(dot_t(every, wkv[0]), gain).astype(BF16).astype(F32)
    new_value = dot_t(every, wkv[1]).astype(BF16).astype(F32)
    own = [jnp.exp(v * math.sqrt(HEAD)) for v in head_sums(query * new_key)]
    own_value = spread([v.astype(BF16).astype(F32) for v in own], new_value.shape) * new_value

    f1.wait()
    picked = dot(sel[...], qz[...].reshape(span, width)).astype(BF16)
    f2s[...] = picked.reshape(nw, slot_dev, width)
    f2 = stage(f2r.at[: nw - 1], [(f2s.at[v], f2r.at[w], w_peer[d]) for d, v in w_at.items()])
    f2r[w] = f2s[w]

    l1.wait()
    l2s[...] = jnp.sum(l1r[...], axis=0)
    l2r[z] = l2s[...]
    l2 = stage(l2r.at[: nz - 1], [(l2s, l2r.at[z], p) for p in z_peer.values()])

    local["cache"].wait()
    f2.wait()
    q_slot = jnp.sum(f2r[...].astype(F32), axis=0) * math.sqrt(HEAD)
    reach = GROUP * cap
    place = lanes((GROUP, reach))
    half = slot_dev // 2
    r1 = []
    for g in range(slot_dev // GROUP):
        part = slice(g * GROUP, (g + 1) * GROUP)
        inside = place - rows_of((GROUP, reach)) * cap
        valid = jnp.logical_and(inside >= 0, inside < size[part].astype(jnp.int32))
        num, den = attend(
            q_slot[part],
            side_by_side(ks, g * GROUP, (g + 1) * GROUP),
            side_by_side(vs, g * GROUP, (g + 1) * GROUP),
            valid,
        )
        acc[part, :width] = num
        acc[part, width - 64 :] = tail_of(acc[part, width - 64 :], den)
        if (g + 1) * GROUP % half == 0:
            done = pl.ds((g + 1) * GROUP - half, half)
            r1s[done] = acc[done].astype(BF16)
            r1.append(
                stage(
                    r1r.at[: nw - 1, done],
                    [(r1s.at[done], r1r.at[w, done], p) for p in w_peer.values()],
                )
            )
    r1r[w] = r1s[...]

    local["rate"].wait()
    local["wo"].wait()
    rate = rate_v[...].reshape(1, depth)

    def attended(sums, lo, hi):
        own_part = [v[lo:hi] for v in own]
        under = [a + b for a, b in zip(columns_of(sums[:, width - 64 :], heads), own_part, strict=True)]
        return ((sums[:, :width] + own_value[lo:hi]) / spread(under, (hi - lo, width))).astype(BF16)

    def updated(proj, lo, hi):
        update = state[lo:hi] + rate * (row_unit(proj) - state[lo:hi])
        result = row_unit(update)
        return pltpu.roll(result, lax.rem(depth - t * width, depth), 1)[:, :width]

    l2.wait()
    x3s[...] = dot(attended(jnp.sum(l2r[...], axis=0), ns, ns + LROWS), wo[...])
    x3r[t] = x3s[...]
    x3 = stage(x3r.at[: nx - 1], [(x3s, x3r.at[t], p) for p in x_peer.values()])

    for part in r1:
        part.wait()
    back = dot(sel_t[:, c].reshape(nz * ns, nw * slot_dev), r1r[...].reshape(nw * slot_dev, width + 64))
    r2s[...] = back.astype(BF16).reshape(nz, ns, width + 64)
    r2 = stage(
        r2r.at[: nz - 1], [(r2s.at[lax.rem(z + d, nz)], r2r.at[z], p) for d, p in z_peer.items()]
    )
    r2r[z] = r2s[z]

    x3.wait()
    out_l[...] = updated(jnp.sum(x3r[...], axis=0), ns, ns + LROWS)[:long_count].astype(BF16)

    r2.wait()
    sums = jnp.sum(r2r[...].astype(F32), axis=0)
    x2s[...] = dot(attended(sums, 0, ns), wo[...]).astype(BF16)
    x2r[t] = x2s[...]
    x2 = stage(x2r.at[: nx - 1], [(x2s, x2r.at[t], p) for p in x_peer.values()])
    x2.wait()
    out_s[...] = updated(jnp.sum(x2r[...].astype(F32), axis=0), 0, ns).astype(BF16)

    for part in sent:
        part.wait()


def hand_over(a_s, a_l, out_s, out_l, sem):
    copies = [
        pltpu.make_async_copy(a_s, out_s, sem.at[0]),
        pltpu.make_async_copy(a_l, out_l, sem.at[1]),
    ]
    for copy in copies:
        copy.start()
    for copy in copies:
        copy.wait()


def on_device(
    sizes,
    short_hidden, long_hidden, short_len, short_slot, w_query, w_key, w_value, w_out, qk_gain, step_rate,
    short_keys, short_values, long_keys, long_values,
):
    ny, nz, nc, nx = sizes
    nw = ny * nc
    ns, width = short_hidden.shape
    long_count = long_hidden.shape[0]
    depth = w_query.shape[0]
    slot_dev = short_keys.shape[0]
    wide = width + 64
    total = short_slot.shape[0]
    span = nz * nc * ns
    dma = pltpu.SemaphoreType.DMA
    args = (
        short_hidden, long_hidden, short_len.reshape(total // 128, 128), short_slot.reshape(total // 128, 128),
        w_query.T, w_key.T, w_value.T, w_out, qk_gain, step_rate,
        *(a.transpose(0, 2, 1) for a in (short_keys, short_values, long_keys, long_values)),
    )
    vmem = pltpu.VMEM
    scratch = [
        vmem((nx, ns, width), BF16), vmem((nx, long_count, width), BF16),
        vmem((2, total // 128, 128), jnp.int32), vmem((width, depth), BF16), vmem((2, width, depth), BF16),
        vmem((width, depth), BF16), vmem((width,), F32), vmem((depth,), F32),
        vmem((2, *args[10].shape), BF16), vmem((2, *args[12].shape), BF16),
        vmem((nw * slot_dev, span), BF16), vmem((nz, nc, ns, nw * slot_dev), BF16),
        vmem((nz, nc, ns, width), BF16),
        vmem((nw, slot_dev, width), BF16), vmem((nw, slot_dev, width), BF16),
        vmem((slot_dev, wide), BF16), vmem((nw, slot_dev, wide), BF16),
        vmem((nz, ns, wide), BF16), vmem((nz, ns, wide), BF16), vmem((slot_dev, wide), F32),
        vmem((LROWS, wide), F32), vmem((nw, LROWS, wide), F32),
        vmem((LROWS, wide), F32), vmem((nz, LROWS, wide), F32),
        vmem((ns, depth), BF16), vmem((nx, ns, depth), BF16),
        vmem((LROWS, depth), F32), vmem((nx, LROWS, depth), F32),
        dma((10,)), dma((12,)), dma((12,)),
    ]
    results = pl.pallas_call(
        functools.partial(kernel, sizes),
        out_shape=(vmem(short_hidden.shape, BF16), vmem(long_hidden.shape, BF16)),
        in_specs=[pl.BlockSpec(memory_space=pl.ANY)] * len(args),
        out_specs=(pl.BlockSpec(memory_space=vmem), pl.BlockSpec(memory_space=vmem)),
        scratch_shapes=scratch,
        compiler_params=pltpu.CompilerParams(collective_id=0, has_side_effects=True),
    )(*args)
    return pl.pallas_call(
        hand_over,
        out_shape=tuple(jax.ShapeDtypeStruct(a.shape, a.dtype) for a in results),
        in_specs=[pl.BlockSpec(memory_space=vmem)] * 2,
        out_specs=(pl.BlockSpec(memory_space=pl.ANY), pl.BlockSpec(memory_space=pl.ANY)),
        scratch_shapes=[dma((2,))],
    )(*(pltpu.with_memory_space_constraint(a, pltpu.VMEM) for a in results))


def solution(mesh):
    sizes = (*GRID[mesh.shape["seq"]], mesh.shape["tp"])
    return jax.shard_map(
        functools.partial(on_device, sizes),
        mesh=mesh,
        in_specs=(
            P("seq", "tp"),
            P(None, "tp"),
            P(),
            P(),
            P(None, "tp"),
            P(None, "tp"),
            P(None, "tp"),
            P("tp", None),
            P("tp"),
            P(),
            P("seq", None, "tp"),
            P("seq", None, "tp"),
            P(None, "seq", "tp"),
            P(None, "seq", "tp"),
        ),
        out_specs=(P("seq", "tp"), P(None, "tp")),
        check_vma=False,
    )
```

```python
import functools
import math

import jax
import jax.numpy as jnp
from jax import lax
from jax.experimental import pallas as pl
from jax.experimental.pallas import tpu as pltpu
from jax.sharding import PartitionSpec as P

HEAD = 64
EPS = 1e-06
MESH = pl.DeviceIdType.MESH
F32 = jnp.float32
BF16 = jnp.bfloat16
GRID = {64: (4, 8, 2), 8: (2, 2, 2)}
GROUP = 8
LROWS = 8


def dot(a, b):
    return lax.dot_general(a, b, (((1,), (0,)), ((), ())), preferred_element_type=F32)


def dot_t(a, b):
    return lax.dot_general(a, b, (((1,), (1,)), ((), ())), preferred_element_type=F32)


def lanes(shape):
    return lax.broadcasted_iota(jnp.int32, shape, 1)


def rows_of(shape):
    return lax.broadcasted_iota(jnp.int32, shape, 0)


def head_sums(x):
    head = lanes(x.shape) // HEAD
    return [
        jnp.sum(jnp.where(head == h, x, 0.0), axis=1, keepdims=True)
        for h in range(x.shape[1] // HEAD)
    ]


def spread(columns, shape):
    head = lanes(shape) // HEAD
    out = jnp.broadcast_to(columns[0], shape)
    for h in range(1, len(columns)):
        out = jnp.where(head == h, columns[h], out)
    return out


def head_unit(x, gain):
    scale = [lax.rsqrt(s + EPS) for s in head_sums(x * x)]
    return x * spread(scale, x.shape) * gain


def row_unit(x):
    return x * lax.rsqrt(jnp.sum(x * x, axis=1, keepdims=True) * (1.0 / x.shape[1]) + EPS)


def by_head(q):
    head = lanes(q.shape) // HEAD
    return jnp.concatenate(
        [jnp.where(head == h, q, 0.0) for h in range(q.shape[1] // HEAD)], axis=0
    ).astype(BF16)


def attend(q, keys, values, valid):
    r, width = q.shape
    heads = width // HEAD
    scores = dot(by_head(q), keys)
    weights = jnp.where(jnp.concatenate([valid] * heads, axis=0), jnp.exp(scores), 0.0)
    den = jnp.sum(weights, axis=1, keepdims=True)
    full = dot_t(weights.astype(BF16), values)
    head = lanes((r, width)) // HEAD
    num = full[:r]
    for h in range(1, heads):
        num = jnp.where(head == h, full[h * r : (h + 1) * r], num)
    return num, [den[h * r : (h + 1) * r] for h in range(heads)]


def tail_of(part, columns):
    half = part.shape[1] // 2
    lane = lanes(part.shape)
    out = jnp.where(lane < half, part, 0.0)
    for h, column in enumerate(columns):
        out = jnp.where(lane == half + h, column, out)
    return out


def columns_of(tail, heads):
    half = tail.shape[1] // 2
    lane = lanes(tail.shape)
    return [
        jnp.sum(jnp.where(lane == half + h, tail, 0.0), axis=1, keepdims=True)
        for h in range(heads)
    ]


def side_by_side(ref, lo, hi):
    return jnp.concatenate([ref[i] for i in range(lo, hi)], axis=1)


def far_first(n):
    return sorted(range(1, n), key=lambda d: -min(d, n - d))


def kernel(
    sizes,
    hid_s, hid_l, len_h, slot_h, wq_h, wk_h, wv_h, wo_h, gain_h, rate_h, ks_h, vs_h, kl_h, vl_h,
    out_s, out_l,
    hbuf, hlbuf, index_v, wq, wkv, wo, gain_v, rate_v, cache_v, long_v,
    sel, sel_t, qz, f2s, f2r, r1s, r1r, r2s, r2r, acc, l1s, l1r, l2s, l2r, x2s, x2r, x3s, x3r,
    local_sem, send_sem, recv_sem, ready_sem,
):
    ny, nz, nc, nx = sizes
    nw = ny * nc
    ns, width = hid_s.shape
    long_count = hid_l.shape[0]
    depth = wq_h.shape[1]
    heads = width // HEAD
    slot_dev, cap = ks_h.shape[0], ks_h.shape[2]
    total_rows = slot_h.shape[0]
    s = lax.axis_index("seq")
    t = lax.axis_index("tp")
    c = lax.rem(s, nc)
    z = lax.rem(s // nc, nz)
    y = s // (nc * nz)
    w = y * nc + c

    def at(y_, z_, c_, t_):
        return {"seq": (y_ * nz + z_) * nc + c_, "tp": t_}

    x_peer = {d: at(y, z, c, lax.rem(t + d, nx)) for d in far_first(nx)}
    z_peer = {d: at(y, lax.rem(z + d, nz), c, t) for d in far_first(nz)}
    w_at = {d: lax.rem(w + d, nw) for d in far_first(nw)}
    w_peer = {d: at(v // nc, z, lax.rem(v, nc), t) for d, v in w_at.items()}

    barrier = pltpu.get_barrier_semaphore()
    partner = at(y, z, 1 - c, t)

    def signal(sem, peer):
        pl.semaphore_signal(sem, inc=1, device_id=peer, device_id_type=MESH)

    for d in far_first(nx):
        signal(barrier, at(y, z, 0, lax.rem(t + d, nx)))
    for d in far_first(ny):
        signal(barrier, at(lax.rem(y + d, ny), z, 0, t))
    for d in far_first(nz):
        signal(barrier, at(y, lax.rem(z + d, nz), 1, t))

    @pl.when(c == 1)
    def _():
        signal(barrier, partner)

    local = {}
    for i, (name, dst, *srcs) in enumerate((
        ("hs", hbuf.at[t], hid_s), ("index", index_v, slot_h, len_h), ("gain", gain_v, gain_h), ("wq", wq, wq_h),
        ("hl", hlbuf.at[t], hid_l), ("long", long_v, kl_h, vl_h), ("wkv", wkv, wk_h, wv_h), ("cache", cache_v, ks_h, vs_h),
        ("wo", wo, wo_h), ("rate", rate_v, rate_h),
    )):
        for k, src in enumerate(srcs):
            pltpu.make_async_copy(src, dst.at[k] if len(srcs) > 1 else dst, local_sem.at[i]).start()
        local[name] = pltpu.make_async_copy(dst, dst, local_sem.at[i])
    kl, vl = long_v.at[0], long_v.at[1]
    ks, vs = cache_v.at[0], cache_v.at[1]
    slot_v, len_v = index_v.at[0], index_v.at[1]

    sent = []

    def stage(blocks, copies):
        k = len(sent)
        for src, dst, peer in copies:
            pltpu.make_async_remote_copy(
                src_ref=src, dst_ref=dst, send_sem=send_sem.at[k], recv_sem=recv_sem.at[k],
                device_id=peer, device_id_type=MESH,
            ).start()
        sent.append(pltpu.make_async_copy(blocks, blocks, send_sem.at[k]))
        return pltpu.make_async_copy(blocks, blocks, recv_sem.at[k])

    @pl.when(c == 0)
    def _():
        pl.semaphore_wait(barrier, nc * (nx - 1 + ny - 1) + 1)
        signal(ready_sem, partner)

    @pl.when(c == 1)
    def _():
        pl.semaphore_wait(ready_sem, 1)

    x1 = stage(hbuf.at[: nx - 1], [(hid_s, hbuf.at[t], p) for p in x_peer.values()])
    x1l = stage(hlbuf.at[: nx - 1], [(hid_l, hlbuf.at[t], p) for p in x_peer.values()])

    qz[:, 1 - c] = jnp.zeros((nz, ns, width), BF16)
    local["index"].wait()
    span = nz * nc * ns
    per = 128 // (nc * ns)
    ids = rows_of((nw * slot_dev, 128))
    ids = ids // (nc * slot_dev) * (nz * nc * slot_dev) + z * (nc * slot_dev) + lax.rem(ids, nc * slot_dev)
    for i in range(span // 128):
        row = slot_v[pl.ds(y * (span // 128) + i, 1), :]
        hit = jnp.where(ids == row, 1.0, 0.0)
        sel[:, i * 128 : (i + 1) * 128] = hit.astype(BF16)
        sel_t[i * per : (i + 1) * per] = (
            jnp.transpose(hit).astype(BF16).reshape(per, nc, ns, nw * slot_dev)
        )
    mine = rows_of((slot_dev, 128)) + s * slot_dev
    size = jnp.zeros((slot_dev, 128), F32)
    for i in range(total_rows):
        size += jnp.where(mine == slot_v[i : i + 1, :], len_v[i : i + 1, :].astype(F32), 0.0)
    size = jnp.sum(size, axis=1, keepdims=True)

    for name in ("hs", "gain", "wq"):
        local[name].wait()
    x1.wait()
    gain = gain_v[...].reshape(1, width)
    hidden = jnp.concatenate([hbuf[i] for i in range(nx)], axis=1)
    q_short = head_unit(dot_t(hidden, wq[...]), gain).astype(BF16)
    qz[z, c] = q_short
    @pl.when(c == 1)
    def _():
        pl.semaphore_wait(barrier, nc * (nz - 1))
        signal(ready_sem, partner)

    @pl.when(c == 0)
    def _():
        pl.semaphore_wait(ready_sem, 1)

    f1 = stage(qz.at[: nz - 1, c], [(qz.at[z, c], qz.at[z, c], p) for p in z_peer.values()])

    local["hl"].wait()
    x1l.wait()
    hidden_l = jnp.concatenate([hlbuf[i].astype(F32) for i in range(nx)], axis=1)
    hidden_l = jnp.concatenate([hidden_l, jnp.zeros((LROWS - long_count, depth), F32)], axis=0)
    q_long = head_unit(dot_t(hidden_l.astype(BF16), wq[...]), gain).astype(BF16)
    local["long"].wait()
    positions = kl.shape[0] * kl.shape[2]
    valid = lanes((LROWS, positions)) // kl.shape[2] == rows_of((LROWS, positions))
    num, den = attend(
        q_long.astype(F32) * math.sqrt(HEAD),
        side_by_side(kl, 0, long_count),
        side_by_side(vl, 0, long_count),
        valid,
    )
    l1s[:, :width] = num
    l1s[:, width - 64 :] = tail_of(l1s[:, width - 64 :], den)
    l1r[w] = l1s[...]
    l1 = stage(l1r.at[: nw - 1], [(l1s, l1r.at[w], p) for p in w_peer.values()])

    local["wkv"].wait()
    state = jnp.concatenate([hidden.astype(F32), hidden_l], axis=0)
    every = state.astype(BF16)
    query = jnp.concatenate([q_short.astype(F32), q_long.astype(F32)], axis=0)
    new_key = head_unit(dot_t(every, wkv[0]), gain).astype(BF16).astype(F32)
    new_value = dot_t(every, wkv[1]).astype(BF16).astype(F32)
    own = [jnp.exp(v * math.sqrt(HEAD)) for v in head_sums(query * new_key)]
    own_value = spread([v.astype(BF16).astype(F32) for v in own], new_value.shape) * new_value

    f1.wait()
    picked = dot(sel[...], qz[...].reshape(span, width)).astype(BF16)
    f2s[...] = picked.reshape(nw, slot_dev, width)
    f2 = stage(f2r.at[: nw - 1], [(f2s.at[v], f2r.at[w], w_peer[d]) for d, v in w_at.items()])
    f2r[w] = f2s[w]

    l1.wait()
    l2s[...] = jnp.sum(l1r[...], axis=0)
    l2r[z] = l2s[...]
    l2 = stage(l2r.at[: nz - 1], [(l2s, l2r.at[z], p) for p in z_peer.values()])

    local["cache"].wait()
    f2.wait()
    q_slot = jnp.sum(f2r[...].astype(F32), axis=0) * math.sqrt(HEAD)
    reach = GROUP * cap
    place = lanes((GROUP, reach))
    half = slot_dev // 2
    r1 = []
    for g in range(slot_dev // GROUP):
        part = slice(g * GROUP, (g + 1) * GROUP)
        inside = place - rows_of((GROUP, reach)) * cap
        valid = jnp.logical_and(inside >= 0, inside < size[part].astype(jnp.int32))
        num, den = attend(
            q_slot[part],
            side_by_side(ks, g * GROUP, (g + 1) * GROUP),
            side_by_side(vs, g * GROUP, (g + 1) * GROUP),
            valid,
        )
        acc[part, :width] = num
        acc[part, width - 64 :] = tail_of(acc[part, width - 64 :], den)
        if (g + 1) * GROUP % half == 0:
            done = pl.ds((g + 1) * GROUP - half, half)
            r1s[done] = acc[done].astype(BF16)
            r1.append(
                stage(
                    r1r.at[: nw - 1, done],
                    [(r1s.at[done], r1r.at[w, done], p) for p in w_peer.values()],
                )
            )
    r1r[w] = r1s[...]

    local["rate"].wait()
    local["wo"].wait()
    rate = rate_v[...].reshape(1, depth)

    def attended(sums, lo, hi):
        own_part = [v[lo:hi] for v in own]
        under = [a + b for a, b in zip(columns_of(sums[:, width - 64 :], heads), own_part, strict=True)]
        return ((sums[:, :width] + own_value[lo:hi]) / spread(under, (hi - lo, width))).astype(BF16)

    def updated(proj, lo, hi):
        update = state[lo:hi] + rate * (row_unit(proj) - state[lo:hi])
        result = row_unit(update)
        return pltpu.roll(result, lax.rem(depth - t * width, depth), 1)[:, :width]

    l2.wait()
    x3s[...] = dot(attended(jnp.sum(l2r[...], axis=0), ns, ns + LROWS), wo[...])
    x3r[t] = x3s[...]
    x3 = stage(x3r.at[: nx - 1], [(x3s, x3r.at[t], p) for p in x_peer.values()])

    for part in r1:
        part.wait()
    back = dot(sel_t[:, c].reshape(nz * ns, nw * slot_dev), r1r[...].reshape(nw * slot_dev, width + 64))
    r2s[...] = back.astype(BF16).reshape(nz, ns, width + 64)
    r2 = stage(
        r2r.at[: nz - 1], [(r2s.at[lax.rem(z + d, nz)], r2r.at[z], p) for d, p in z_peer.items()]
    )
    r2r[z] = r2s[z]

    x3.wait()
    out_l[...] = updated(jnp.sum(x3r[...], axis=0), ns, ns + LROWS)[:long_count].astype(BF16)

    r2.wait()
    sums = jnp.sum(r2r[...].astype(F32), axis=0)
    x2s[...] = dot(attended(sums, 0, ns), wo[...]).astype(BF16)
    x2r[t] = x2s[...]
    x2 = stage(x2r.at[: nx - 1], [(x2s, x2r.at[t], p) for p in x_peer.values()])
    x2.wait()
    out_s[...] = updated(jnp.sum(x2r[...].astype(F32), axis=0), 0, ns).astype(BF16)

    for part in sent:
        part.wait()


def hand_over(a_s, a_l, out_s, out_l, sem):
    copies = [
        pltpu.make_async_copy(a_s, out_s, sem.at[0]),
        pltpu.make_async_copy(a_l, out_l, sem.at[1]),
    ]
    for copy in copies:
        copy.start()
    for copy in copies:
        copy.wait()


def on_device(
    sizes,
    short_hidden, long_hidden, short_len, short_slot, w_query, w_key, w_value, w_out, qk_gain, step_rate,
    short_keys, short_values, long_keys, long_values,
):
    ny, nz, nc, nx = sizes
    nw = ny * nc
    ns, width = short_hidden.shape
    long_count = long_hidden.shape[0]
    depth = w_query.shape[0]
    slot_dev = short_keys.shape[0]
    wide = width + 64
    total = short_slot.shape[0]
    span = nz * nc * ns
    dma = pltpu.SemaphoreType.DMA
    args = (
        short_hidden, long_hidden, short_len.reshape(total // 128, 128), short_slot.reshape(total // 128, 128),
        w_query.T, w_key.T, w_value.T, w_out, qk_gain, step_rate,
        *(a.transpose(0, 2, 1) for a in (short_keys, short_values, long_keys, long_values)),
    )
    vmem = pltpu.VMEM
    scratch = [
        vmem((nx, ns, width), BF16), vmem((nx, long_count, width), BF16),
        vmem((2, total // 128, 128), jnp.int32), vmem((width, depth), BF16), vmem((2, width, depth), BF16),
        vmem((width, depth), BF16), vmem((width,), F32), vmem((depth,), F32),
        vmem((2, *args[10].shape), BF16), vmem((2, *args[12].shape), BF16),
        vmem((nw * slot_dev, span), BF16), vmem((nz, nc, ns, nw * slot_dev), BF16),
        vmem((nz, nc, ns, width), BF16),
        vmem((nw, slot_dev, width), BF16), vmem((nw, slot_dev, width), BF16),
        vmem((slot_dev, wide), BF16), vmem((nw, slot_dev, wide), BF16),
        vmem((nz, ns, wide), BF16), vmem((nz, ns, wide), BF16), vmem((slot_dev, wide), F32),
        vmem((LROWS, wide), F32), vmem((nw, LROWS, wide), F32),
        vmem((LROWS, wide), F32), vmem((nz, LROWS, wide), F32),
        vmem((ns, depth), BF16), vmem((nx, ns, depth), BF16),
        vmem((LROWS, depth), F32), vmem((nx, LROWS, depth), F32),
        dma((10,)), dma((12,)), dma((12,)), pltpu.SemaphoreType.REGULAR,
    ]
    results = pl.pallas_call(
        functools.partial(kernel, sizes),
        out_shape=(vmem(short_hidden.shape, BF16), vmem(long_hidden.shape, BF16)),
        in_specs=[pl.BlockSpec(memory_space=pl.ANY)] * len(args),
        out_specs=(pl.BlockSpec(memory_space=vmem), pl.BlockSpec(memory_space=vmem)),
        scratch_shapes=scratch,
        compiler_params=pltpu.CompilerParams(collective_id=0, has_side_effects=True),
    )(*args)
    return pl.pallas_call(
        hand_over,
        out_shape=tuple(jax.ShapeDtypeStruct(a.shape, a.dtype) for a in results),
        in_specs=[pl.BlockSpec(memory_space=vmem)] * 2,
        out_specs=(pl.BlockSpec(memory_space=pl.ANY), pl.BlockSpec(memory_space=pl.ANY)),
        scratch_shapes=[dma((2,))],
    )(*(pltpu.with_memory_space_constraint(a, pltpu.VMEM) for a in results))


def solution(mesh):
    sizes = (*GRID[mesh.shape["seq"]], mesh.shape["tp"])
    return jax.shard_map(
        functools.partial(on_device, sizes),
        mesh=mesh,
        in_specs=(
            P("seq", "tp"),
            P(None, "tp"),
            P(),
            P(),
            P(None, "tp"),
            P(None, "tp"),
            P(None, "tp"),
            P("tp", None),
            P("tp"),
            P(),
            P("seq", None, "tp"),
            P("seq", None, "tp"),
            P(None, "seq", "tp"),
            P(None, "seq", "tp"),
        ),
        out_specs=(P("seq", "tp"), P(None, "tp")),
        check_vma=False,
    )
```

```python
import functools
import math

import jax
import jax.numpy as jnp
from jax import lax
from jax.experimental import pallas as pl
from jax.experimental.pallas import tpu as pltpu
from jax.sharding import PartitionSpec as P

HEAD = 64
EPS = 1e-06
MESH = pl.DeviceIdType.MESH
F32 = jnp.float32
BF16 = jnp.bfloat16
GRID = {64: (4, 8, 2), 8: (2, 2, 2)}
GROUP = 8
LROWS = 8


def dot(a, b):
    return lax.dot_general(a, b, (((1,), (0,)), ((), ())), preferred_element_type=F32)


def dot_t(a, b):
    return lax.dot_general(a, b, (((1,), (1,)), ((), ())), preferred_element_type=F32)


def lanes(shape):
    return lax.broadcasted_iota(jnp.int32, shape, 1)


def rows_of(shape):
    return lax.broadcasted_iota(jnp.int32, shape, 0)


def head_sums(x):
    head = lanes(x.shape) // HEAD
    return [
        jnp.sum(jnp.where(head == h, x, 0.0), axis=1, keepdims=True)
        for h in range(x.shape[1] // HEAD)
    ]


def spread(columns, shape):
    head = lanes(shape) // HEAD
    out = jnp.broadcast_to(columns[0], shape)
    for h in range(1, len(columns)):
        out = jnp.where(head == h, columns[h], out)
    return out


def head_unit(x, gain):
    scale = [lax.rsqrt(s + EPS) for s in head_sums(x * x)]
    return x * spread(scale, x.shape) * gain


def row_unit(x):
    return x * lax.rsqrt(jnp.sum(x * x, axis=1, keepdims=True) * (1.0 / x.shape[1]) + EPS)


def by_head(q):
    head = lanes(q.shape) // HEAD
    return jnp.concatenate(
        [jnp.where(head == h, q, 0.0) for h in range(q.shape[1] // HEAD)], axis=0
    ).astype(BF16)


def attend(q, keys, values, valid):
    r, width = q.shape
    heads = width // HEAD
    scores = dot(by_head(q), keys)
    weights = jnp.where(jnp.concatenate([valid] * heads, axis=0), jnp.exp(scores), 0.0)
    den = jnp.sum(weights, axis=1, keepdims=True)
    full = dot_t(weights.astype(BF16), values)
    head = lanes((r, width)) // HEAD
    num = full[:r]
    for h in range(1, heads):
        num = jnp.where(head == h, full[h * r : (h + 1) * r], num)
    return num, [den[h * r : (h + 1) * r] for h in range(heads)]


def attend_slots(query, ks, vs, size, out, lo, hi):
    width, cap = ks.shape[1], ks.shape[2]
    main, heads = width - HEAD, width // HEAD
    reach, groups = GROUP * cap, (hi - lo) // GROUP
    place = lanes((GROUP, reach)) - rows_of((GROUP, reach)) * cap
    live, keys_end, values_end, sums, dens = [], [], [], [], []
    for g in range(groups):
        first = lo + g * GROUP
        part = slice(first, first + GROUP)
        keys, values = (side_by_side(ref, first, first + GROUP) for ref in (ks, vs))
        keys_end.append(keys[main:])
        values_end.append(values[main:])
        live.append(jnp.logical_and(place >= 0, place < size[part].astype(jnp.int32)))
        scores = dot(by_head(query[part, :main]), keys[:main])
        mask = jnp.concatenate([live[g]] * (heads - 1), axis=0)
        weights = jnp.where(mask, jnp.exp(scores), 0.0)
        dens.append(jnp.sum(weights, axis=1, keepdims=True))
        full = dot_t(weights.astype(BF16), values[:main])
        head = lanes((GROUP, main)) // HEAD
        num = full[:GROUP]
        for h in range(1, heads - 1):
            num = jnp.where(head == h, full[h * GROUP : (h + 1) * GROUP], num)
        sums.append(num)
    end = jnp.concatenate([query[lo:hi, main:]] * groups, axis=1)
    end = jnp.where(lanes(end.shape) // HEAD == rows_of(end.shape) // GROUP, end, 0.0).astype(BF16)
    scores = dot(end, jnp.concatenate(keys_end, axis=0))
    weights = jnp.where(jnp.concatenate(live, axis=0), jnp.exp(scores), 0.0)
    den_end = jnp.sum(weights, axis=1, keepdims=True)
    full = dot_t(weights.astype(BF16), jnp.concatenate(values_end, axis=0))
    lane = lanes((GROUP, HEAD))
    rows = []
    for g in range(groups):
        part = slice(g * GROUP, (g + 1) * GROUP)
        columns = [dens[g][h * GROUP : (h + 1) * GROUP] for h in range(heads - 1)] + [den_end[part]]
        last = jnp.zeros((GROUP, HEAD), F32)
        for h, column in enumerate(columns):
            last = jnp.where(lane == h, column, last)
        rows.append(jnp.concatenate([sums[g], full[part, g * HEAD : (g + 1) * HEAD], last], axis=1))
    out[lo:hi] = jnp.concatenate(rows, axis=0).astype(BF16)


def fold(x):
    r, width = x.shape
    whole = width // 128
    last = x[:, whole * 128 :]
    parts = [x[:, i * 128 : (i + 1) * 128] for i in range(whole)]
    parts.append(jnp.concatenate([last[: r // 2], last[r // 2 :]], axis=1))
    return jnp.concatenate(parts, axis=0).astype(BF16)


def unfold(x, r):
    whole = x.shape[0] // r
    last = x[whole * r :]
    parts = [x[i * r : (i + 1) * r] for i in range(whole)]
    parts.append(jnp.concatenate([last[:, :64], last[:, 64:]], axis=0))
    return jnp.concatenate(parts, axis=1)


def tail_of(part, columns):
    half = part.shape[1] // 2
    lane = lanes(part.shape)
    out = jnp.where(lane < half, part, 0.0)
    for h, column in enumerate(columns):
        out = jnp.where(lane == half + h, column, out)
    return out


def columns_of(tail, heads):
    half = tail.shape[1] // 2
    lane = lanes(tail.shape)
    return [
        jnp.sum(jnp.where(lane == half + h, tail, 0.0), axis=1, keepdims=True)
        for h in range(heads)
    ]


def side_by_side(ref, lo, hi):
    return jnp.concatenate([ref[i] for i in range(lo, hi)], axis=1)


def far_first(n):
    return sorted(range(1, n), key=lambda d: -min(d, n - d))


def kernel(
    sizes,
    hid_s, hid_l, len_h, slot_h, wq_h, wk_h, wv_h, wo_h, gain_h, rate_h, ks_h, vs_h, kl_h, vl_h,
    out_s, out_l,
    hbuf, hlbuf, index_v, wq, wkv, wo, gain_v, rate_v, cache_v, long_v,
    sel, sel_t, qz, f2s, f2r, r1s, r1r, r2s, r2r, acc, l1s, l1r, l2s, l2r, x2s, x2r, x3s, x3r,
    local_sem, send_sem, recv_sem, ready_sem,
):
    ny, nz, nc, nx = sizes
    nw = ny * nc
    ns, width = hid_s.shape
    long_count = hid_l.shape[0]
    depth = wq_h.shape[1]
    heads = width // HEAD
    slot_dev, cap = ks_h.shape[0], ks_h.shape[2]
    total_rows = slot_h.shape[0]
    s = lax.axis_index("seq")
    t = lax.axis_index("tp")
    c = lax.rem(s, nc)
    z = lax.rem(s // nc, nz)
    y = s // (nc * nz)
    w = y * nc + c

    def at(y_, z_, c_, t_):
        return {"seq": (y_ * nz + z_) * nc + c_, "tp": t_}

    x_peer = {d: at(y, z, c, lax.rem(t + d, nx)) for d in far_first(nx)}
    z_peer = {d: at(y, lax.rem(z + d, nz), c, t) for d in far_first(nz)}
    w_at = {
        (d, e): lax.rem(y + d, ny) * nc + lax.rem(c + e, nc)
        for d in [*far_first(ny), 0]
        for e in range(nc)
        if d or e
    }
    w_peer = {d: at(v // nc, z, lax.rem(v, nc), t) for d, v in w_at.items()}

    barrier = pltpu.get_barrier_semaphore()
    partner = at(y, z, 1 - c, t)

    def signal(sem, peer):
        pl.semaphore_signal(sem, inc=1, device_id=peer, device_id_type=MESH)

    for d in far_first(nx):
        signal(barrier, at(y, z, 1, lax.rem(t + d, nx)))
    for d in far_first(ny):
        signal(barrier, at(lax.rem(y + d, ny), z, 1, t))
    for d in far_first(nz):
        signal(barrier, at(y, lax.rem(z + d, nz), 0, t))

    @pl.when(c == 0)
    def _():
        signal(barrier, partner)

    local = {}
    for i, (name, dst, *srcs) in enumerate((
        ("hs", hbuf.at[t], hid_s), ("index", index_v, slot_h, len_h), ("gain", gain_v, gain_h), ("wq", wq, wq_h),
        ("hl", hlbuf.at[t], hid_l), ("long", long_v, kl_h, vl_h), ("wkv", wkv, wk_h, wv_h), ("cache", cache_v, ks_h, vs_h),
        ("wo", wo, wo_h), ("rate", rate_v, rate_h),
    )):
        for k, src in enumerate(srcs):
            pltpu.make_async_copy(src, dst.at[k] if len(srcs) > 1 else dst, local_sem.at[i]).start()
        local[name] = pltpu.make_async_copy(dst, dst, local_sem.at[i])
    kl, vl = long_v.at[0], long_v.at[1]
    ks, vs = cache_v.at[0], cache_v.at[1]
    slot_v, len_v = index_v.at[0], index_v.at[1]

    sent = []

    def stage(blocks, copies):
        k = len(sent)
        for src, dst, peer in copies:
            pltpu.make_async_remote_copy(
                src_ref=src, dst_ref=dst, send_sem=send_sem.at[k], recv_sem=recv_sem.at[k],
                device_id=peer, device_id_type=MESH,
            ).start()
        sent.append(pltpu.make_async_copy(blocks, blocks, send_sem.at[k]))
        return pltpu.make_async_copy(blocks, blocks, recv_sem.at[k])

    @pl.when(c == 1)
    def _():
        pl.semaphore_wait(barrier, nc * (nx - 1 + ny - 1) + 1)
        signal(ready_sem, partner)

    @pl.when(c == 0)
    def _():
        pl.semaphore_wait(ready_sem, 1)

    x1 = stage(hbuf.at[: nx - 1], [(hid_s, hbuf.at[t], p) for p in x_peer.values()])
    x1l = stage(hlbuf.at[: nx - 1], [(hid_l, hlbuf.at[t], p) for p in x_peer.values()])

    qz[:, 1 - c] = jnp.zeros((nz, ns, width), BF16)
    local["index"].wait()
    span = nz * nc * ns
    per = 128 // (nc * ns)
    ids = rows_of((nw * slot_dev, 128))
    ids = ids // (nc * slot_dev) * (nz * nc * slot_dev) + z * (nc * slot_dev) + lax.rem(ids, nc * slot_dev)
    for i in range(span // 128):
        row = slot_v[pl.ds(y * (span // 128) + i, 1), :]
        hit = jnp.where(ids == row, 1.0, 0.0)
        sel[:, i * 128 : (i + 1) * 128] = hit.astype(BF16)
        sel_t[i * per : (i + 1) * per] = (
            jnp.transpose(hit).astype(BF16).reshape(per, nc, ns, nw * slot_dev)
        )
    mine = rows_of((slot_dev, 128)) + s * slot_dev
    size = jnp.zeros((slot_dev, 128), F32)
    for i in range(total_rows):
        size += jnp.where(mine == slot_v[i : i + 1, :], len_v[i : i + 1, :].astype(F32), 0.0)
    size = jnp.sum(size, axis=1, keepdims=True)

    @pl.when(c == 0)
    def _():
        pl.semaphore_wait(barrier, nc * (nz - 1))
        signal(ready_sem, partner)

    @pl.when(c == 1)
    def _():
        pl.semaphore_wait(ready_sem, 1)

    for name in ("hs", "gain", "wq"):
        local[name].wait()
    x1.wait()
    gain = gain_v[...].reshape(1, width)
    hidden = jnp.concatenate([hbuf[i] for i in range(nx)], axis=1)
    q_short = head_unit(dot_t(hidden, wq[...]), gain).astype(BF16)
    qz[z, c] = q_short
    f1 = stage(qz.at[: nz - 1, c], [(qz.at[z, c], qz.at[z, c], p) for p in z_peer.values()])

    local["hl"].wait()
    x1l.wait()
    hidden_l = jnp.concatenate([hlbuf[i].astype(F32) for i in range(nx)], axis=1)
    hidden_l = jnp.concatenate([hidden_l, jnp.zeros((LROWS - long_count, depth), F32)], axis=0)
    q_long = head_unit(dot_t(hidden_l.astype(BF16), wq[...]), gain).astype(BF16)
    local["long"].wait()
    positions = kl.shape[0] * kl.shape[2]
    valid = lanes((LROWS, positions)) // kl.shape[2] == rows_of((LROWS, positions))
    num, den = attend(
        q_long.astype(F32) * math.sqrt(HEAD),
        side_by_side(kl, 0, long_count),
        side_by_side(vl, 0, long_count),
        valid,
    )
    l1s[:, :width] = num
    l1s[:, width - 64 :] = tail_of(l1s[:, width - 64 :], den)
    l1r[w] = l1s[...]
    l1 = stage(l1r.at[: nw - 1], [(l1s, l1r.at[w], p) for p in w_peer.values()])

    local["wkv"].wait()
    state = jnp.concatenate([hidden.astype(F32), hidden_l], axis=0)
    every = state.astype(BF16)
    query = jnp.concatenate([q_short.astype(F32), q_long.astype(F32)], axis=0)
    new_key = head_unit(dot_t(every, wkv[0]), gain).astype(BF16).astype(F32)
    new_value = dot_t(every, wkv[1]).astype(BF16).astype(F32)
    own = [jnp.exp(v * math.sqrt(HEAD)) for v in head_sums(query * new_key)]
    own_value = spread([v.astype(BF16).astype(F32) for v in own], new_value.shape) * new_value

    f1.wait()
    picked = dot(sel[...], qz[...].reshape(span, width))
    for u in range(nw):
        f2s[u] = fold(picked[u * slot_dev : (u + 1) * slot_dev])
    f2 = stage(f2r.at[: nw - 1], [(f2s.at[v], f2r.at[w], w_peer[d]) for d, v in w_at.items()])
    f2r[w] = f2s[w]

    l1.wait()
    l2s[...] = jnp.sum(l1r[...], axis=0)
    l2r[z] = l2s[...]
    l2 = stage(l2r.at[: nz - 1], [(l2s, l2r.at[z], p) for p in z_peer.values()])

    local["cache"].wait()
    f2.wait()
    q_slot = unfold(jnp.sum(f2r[...].astype(F32), axis=0), slot_dev) * math.sqrt(HEAD)
    half = slot_dev // 2
    r1 = [
        stage(
            r1r.at[: nw - 1, pl.ds(lo, half)],
            [(r1s.at[pl.ds(lo, half)], r1r.at[w, pl.ds(lo, half)], p) for p in w_peer.values()],
        )
        for lo in range(0, slot_dev, half)
        if attend_slots(q_slot, ks, vs, size, r1s, lo, lo + half) is None
    ]
    r1r[w] = r1s[...]

    local["rate"].wait()
    local["wo"].wait()
    rate = rate_v[...].reshape(1, depth)

    def attended(sums, lo, hi):
        own_part = [v[lo:hi] for v in own]
        under = [a + b for a, b in zip(columns_of(sums[:, width - 64 :], heads), own_part, strict=True)]
        return ((sums[:, :width] + own_value[lo:hi]) / spread(under, (hi - lo, width))).astype(BF16)

    def updated(proj, lo, hi):
        update = state[lo:hi] + rate * (row_unit(proj) - state[lo:hi])
        result = row_unit(update)
        return pltpu.roll(result, lax.rem(depth - t * width, depth), 1)[:, :width]

    l2.wait()
    x3s[...] = dot(attended(jnp.sum(l2r[...], axis=0), ns, ns + LROWS), wo[...])
    x3r[t] = x3s[...]
    x3 = stage(x3r.at[: nx - 1], [(x3s, x3r.at[t], p) for p in x_peer.values()])

    for part in r1:
        part.wait()
    back = dot(sel_t[:, c].reshape(nz * ns, nw * slot_dev), r1r[...].reshape(nw * slot_dev, width + 64))
    r2s[...] = back.astype(BF16).reshape(nz, ns, width + 64)
    r2 = stage(
        r2r.at[: nz - 1], [(r2s.at[lax.rem(z + d, nz)], r2r.at[z], p) for d, p in z_peer.items()]
    )
    r2r[z] = r2s[z]

    x3.wait()
    out_l[...] = updated(jnp.sum(x3r[...], axis=0), ns, ns + LROWS)[:long_count].astype(BF16)

    r2.wait()
    sums = jnp.sum(r2r[...].astype(F32), axis=0)
    x2s[...] = dot(attended(sums, 0, ns), wo[...]).astype(BF16)
    x2r[t] = x2s[...]
    x2 = stage(x2r.at[: nx - 1], [(x2s, x2r.at[t], p) for p in x_peer.values()])
    x2.wait()
    out_s[...] = updated(jnp.sum(x2r[...].astype(F32), axis=0), 0, ns).astype(BF16)

    for part in sent:
        part.wait()


def hand_over(a_s, a_l, out_s, out_l, sem):
    copies = [
        pltpu.make_async_copy(a_s, out_s, sem.at[0]),
        pltpu.make_async_copy(a_l, out_l, sem.at[1]),
    ]
    for copy in copies:
        copy.start()
    for copy in copies:
        copy.wait()


def on_device(
    sizes,
    short_hidden, long_hidden, short_len, short_slot, w_query, w_key, w_value, w_out, qk_gain, step_rate,
    short_keys, short_values, long_keys, long_values,
):
    ny, nz, nc, nx = sizes
    nw = ny * nc
    ns, width = short_hidden.shape
    long_count = long_hidden.shape[0]
    depth = w_query.shape[0]
    slot_dev = short_keys.shape[0]
    wide = width + 64
    total = short_slot.shape[0]
    span = nz * nc * ns
    dma = pltpu.SemaphoreType.DMA
    args = (
        short_hidden, long_hidden, short_len.reshape(total // 128, 128), short_slot.reshape(total // 128, 128),
        w_query.T, w_key.T, w_value.T, w_out, qk_gain, step_rate,
        *(a.transpose(0, 2, 1) for a in (short_keys, short_values, long_keys, long_values)),
    )
    vmem = pltpu.VMEM
    scratch = [
        vmem((nx, ns, width), BF16), vmem((nx, long_count, width), BF16),
        vmem((2, total // 128, 128), jnp.int32), vmem((width, depth), BF16), vmem((2, width, depth), BF16),
        vmem((width, depth), BF16), vmem((width,), F32), vmem((depth,), F32),
        vmem((2, *args[10].shape), BF16), vmem((2, *args[12].shape), BF16),
        vmem((nw * slot_dev, span), BF16), vmem((nz, nc, ns, nw * slot_dev), BF16),
        vmem((nz, nc, ns, width), BF16),
        *(vmem((nw, slot_dev // 2 * (width // HEAD), 128), BF16) for _ in range(2)),
        vmem((slot_dev, wide), BF16), vmem((nw, slot_dev, wide), BF16),
        vmem((nz, ns, wide), BF16), vmem((nz, ns, wide), BF16), vmem((slot_dev, wide), F32),
        vmem((LROWS, wide), F32), vmem((nw, LROWS, wide), F32),
        vmem((LROWS, wide), F32), vmem((nz, LROWS, wide), F32),
        vmem((ns, depth), BF16), vmem((nx, ns, depth), BF16),
        vmem((LROWS, depth), F32), vmem((nx, LROWS, depth), F32),
        dma((10,)), dma((12,)), dma((12,)), pltpu.SemaphoreType.REGULAR,
    ]
    results = pl.pallas_call(
        functools.partial(kernel, sizes),
        out_shape=(vmem(short_hidden.shape, BF16), vmem(long_hidden.shape, BF16)),
        in_specs=[pl.BlockSpec(memory_space=pl.ANY)] * len(args),
        out_specs=(pl.BlockSpec(memory_space=vmem), pl.BlockSpec(memory_space=vmem)),
        scratch_shapes=scratch,
        compiler_params=pltpu.CompilerParams(collective_id=0, has_side_effects=True),
    )(*args)
    return pl.pallas_call(
        hand_over,
        out_shape=tuple(jax.ShapeDtypeStruct(a.shape, a.dtype) for a in results),
        in_specs=[pl.BlockSpec(memory_space=vmem)] * 2,
        out_specs=(pl.BlockSpec(memory_space=pl.ANY), pl.BlockSpec(memory_space=pl.ANY)),
        scratch_shapes=[dma((2,))],
    )(*(pltpu.with_memory_space_constraint(a, pltpu.VMEM) for a in results))


def solution(mesh):
    sizes = (*GRID[mesh.shape["seq"]], mesh.shape["tp"])
    return jax.shard_map(
        functools.partial(on_device, sizes),
        mesh=mesh,
        in_specs=(
            P("seq", "tp"),
            P(None, "tp"),
            P(),
            P(),
            P(None, "tp"),
            P(None, "tp"),
            P(None, "tp"),
            P("tp", None),
            P("tp"),
            P(),
            P("seq", None, "tp"),
            P("seq", None, "tp"),
            P(None, "seq", "tp"),
            P(None, "seq", "tp"),
        ),
        out_specs=(P("seq", "tp"), P(None, "tp")),
        check_vma=False,
    )
```

```python
import functools
import math

import jax
import jax.numpy as jnp
from jax import lax
from jax.experimental import pallas as pl
from jax.experimental.pallas import tpu as pltpu
from jax.sharding import PartitionSpec as P

HEAD = 64
EPS = 1e-06
MESH = pl.DeviceIdType.MESH
F32 = jnp.float32
BF16 = jnp.bfloat16
GRID = {64: (4, 8, 2), 8: (2, 2, 2)}
GROUP = 8
LROWS = 8


def dot(a, b):
    return lax.dot_general(a, b, (((1,), (0,)), ((), ())), preferred_element_type=F32)


def dot_t(a, b):
    return lax.dot_general(a, b, (((1,), (1,)), ((), ())), preferred_element_type=F32)


def lanes(shape):
    return lax.broadcasted_iota(jnp.int32, shape, 1)


def rows_of(shape):
    return lax.broadcasted_iota(jnp.int32, shape, 0)


def head_sums(x):
    head = lanes(x.shape) // HEAD
    return [
        jnp.sum(jnp.where(head == h, x, 0.0), axis=1, keepdims=True)
        for h in range(x.shape[1] // HEAD)
    ]


def spread(columns, shape):
    head = lanes(shape) // HEAD
    out = jnp.broadcast_to(columns[0], shape)
    for h in range(1, len(columns)):
        out = jnp.where(head == h, columns[h], out)
    return out


def head_unit(x, gain):
    scale = [lax.rsqrt(s + EPS) for s in head_sums(x * x)]
    return x * spread(scale, x.shape) * gain


def row_unit(x):
    return x * lax.rsqrt(jnp.sum(x * x, axis=1, keepdims=True) * (1.0 / x.shape[1]) + EPS)


def by_head(q):
    head = lanes(q.shape) // HEAD
    return jnp.concatenate(
        [jnp.where(head == h, q, 0.0) for h in range(q.shape[1] // HEAD)], axis=0
    ).astype(BF16)


def attend(q, keys, values, valid):
    r, width = q.shape
    heads = width // HEAD
    scores = dot(by_head(q), keys)
    weights = jnp.where(jnp.concatenate([valid] * heads, axis=0), jnp.exp(scores), 0.0)
    den = jnp.sum(weights, axis=1, keepdims=True)
    full = dot_t(weights.astype(BF16), values)
    head = lanes((r, width)) // HEAD
    num = full[:r]
    for h in range(1, heads):
        num = jnp.where(head == h, full[h * r : (h + 1) * r], num)
    return num, [den[h * r : (h + 1) * r] for h in range(heads)]


def attend_slots(query, ks, vs, size, out, lo, hi):
    width, cap = ks.shape[1], ks.shape[2]
    main, heads = width - HEAD, width // HEAD
    reach, groups = GROUP * cap, (hi - lo) // GROUP
    place = lanes((GROUP, reach)) - rows_of((GROUP, reach)) * cap
    live, keys_end, values_end, sums, dens = [], [], [], [], []
    for g in range(groups):
        first = lo + g * GROUP
        part = slice(first, first + GROUP)
        keys, values = (side_by_side(ref, first, first + GROUP) for ref in (ks, vs))
        keys_end.append(keys[main:])
        values_end.append(values[main:])
        live.append(jnp.logical_and(place >= 0, place < size[part].astype(jnp.int32)))
        scores = dot(by_head(query[part, :main]), keys[:main])
        mask = jnp.concatenate([live[g]] * (heads - 1), axis=0)
        weights = jnp.where(mask, jnp.exp(scores), 0.0)
        dens.append(jnp.sum(weights, axis=1, keepdims=True))
        full = dot_t(weights.astype(BF16), values[:main])
        head = lanes((GROUP, main)) // HEAD
        num = full[:GROUP]
        for h in range(1, heads - 1):
            num = jnp.where(head == h, full[h * GROUP : (h + 1) * GROUP], num)
        sums.append(num)
    end = jnp.concatenate([query[lo:hi, main:]] * groups, axis=1)
    end = jnp.where(lanes(end.shape) // HEAD == rows_of(end.shape) // GROUP, end, 0.0).astype(BF16)
    scores = dot(end, jnp.concatenate(keys_end, axis=0))
    weights = jnp.where(jnp.concatenate(live, axis=0), jnp.exp(scores), 0.0)
    den_end = jnp.sum(weights, axis=1, keepdims=True)
    full = dot_t(weights.astype(BF16), jnp.concatenate(values_end, axis=0))
    lane = lanes((GROUP, HEAD))
    rows = []
    for g in range(groups):
        part = slice(g * GROUP, (g + 1) * GROUP)
        columns = [dens[g][h * GROUP : (h + 1) * GROUP] for h in range(heads - 1)] + [den_end[part]]
        last = jnp.zeros((GROUP, HEAD), F32)
        for h, column in enumerate(columns):
            last = jnp.where(lane == h, column, last)
        rows.append(jnp.concatenate([sums[g], full[part, g * HEAD : (g + 1) * HEAD], last], axis=1))
    out[lo:hi] = jnp.concatenate(rows, axis=0).astype(BF16)


def fold(x):
    r, width = x.shape
    whole = width // 128
    last = x[:, whole * 128 :]
    parts = [x[:, i * 128 : (i + 1) * 128] for i in range(whole)]
    parts.append(jnp.concatenate([last[: r // 2], last[r // 2 :]], axis=1))
    return jnp.concatenate(parts, axis=0).astype(BF16)


def unfold(x, r):
    whole = x.shape[0] // r
    last = x[whole * r :]
    parts = [x[i * r : (i + 1) * r] for i in range(whole)]
    parts.append(jnp.concatenate([last[:, :64], last[:, 64:]], axis=0))
    return jnp.concatenate(parts, axis=1)


def tail_of(part, columns):
    half = part.shape[1] // 2
    lane = lanes(part.shape)
    out = jnp.where(lane < half, part, 0.0)
    for h, column in enumerate(columns):
        out = jnp.where(lane == half + h, column, out)
    return out


def columns_of(tail, heads):
    half = tail.shape[1] // 2
    lane = lanes(tail.shape)
    return [
        jnp.sum(jnp.where(lane == half + h, tail, 0.0), axis=1, keepdims=True)
        for h in range(heads)
    ]


def side_by_side(ref, lo, hi):
    return jnp.concatenate([ref[i] for i in range(lo, hi)], axis=1)


def far_first(n):
    return sorted(range(1, n), key=lambda d: -min(d, n - d))


def kernel(
    sizes,
    hid_s, hid_l, len_h, slot_h, wq_h, wk_h, wv_h, wo_h, gain_h, rate_h, ks_h, vs_h, kl_h, vl_h,
    out_s, out_l,
    hbuf, hlbuf, index_v, wq, wkv, wo, gain_v, rate_v, cache_v, long_v,
    sel, sel_t, qz, f2s, f2r, r1s, r1r, r2s, r2r, acc, l1s, l1r, l2s, l2r, x2s, x2r, x3s, x3r,
    local_sem, send_sem, recv_sem, ready_sem,
):
    ny, nz, nc, nx = sizes
    nw = ny * nc
    ns, width = hid_s.shape
    long_count = hid_l.shape[0]
    depth = wq_h.shape[1]
    heads = width // HEAD
    slot_dev, cap = ks_h.shape[0], ks_h.shape[2]
    total_rows = slot_h.shape[0]
    s = lax.axis_index("seq")
    t = lax.axis_index("tp")
    c = lax.rem(s, nc)
    z = lax.rem(s // nc, nz)
    y = s // (nc * nz)
    w = y * nc + c

    def at(y_, z_, c_, t_):
        return {"seq": (y_ * nz + z_) * nc + c_, "tp": t_}

    x_peer = {d: at(y, z, c, lax.rem(t + d, nx)) for d in far_first(nx)}
    z_peer = {d: at(y, lax.rem(z + d, nz), c, t) for d in far_first(nz)}
    w_at = {
        (d, e): lax.rem(y + d, ny) * nc + lax.rem(c + e, nc)
        for d in [*far_first(ny), 0]
        for e in range(nc)
        if d or e
    }
    w_peer = {d: at(v // nc, z, lax.rem(v, nc), t) for d, v in w_at.items()}

    barrier = pltpu.get_barrier_semaphore()
    partner = at(y, z, 1 - c, t)

    def signal(sem, peer):
        pl.semaphore_signal(sem, inc=1, device_id=peer, device_id_type=MESH)

    for d in far_first(nx):
        signal(barrier, at(y, z, 1, lax.rem(t + d, nx)))
    for d in far_first(ny):
        signal(barrier, at(lax.rem(y + d, ny), z, 1, t))
    for d in far_first(nz):
        signal(barrier, at(y, lax.rem(z + d, nz), 0, t))

    @pl.when(c == 0)
    def _():
        signal(barrier, partner)

    local = {}
    for i, (name, dst, *srcs) in enumerate((
        ("hs", hbuf.at[t], hid_s), ("index", index_v, slot_h, len_h), ("gain", gain_v, gain_h), ("wq", wq, wq_h),
        ("hl", hlbuf.at[t], hid_l), ("long", long_v, kl_h, vl_h), ("wkv", wkv, wk_h, wv_h), ("cache", cache_v, ks_h, vs_h),
        ("wo", wo, wo_h), ("rate", rate_v, rate_h),
    )):
        for k, src in enumerate(srcs):
            pltpu.make_async_copy(src, dst.at[k] if len(srcs) > 1 else dst, local_sem.at[i]).start()
        local[name] = pltpu.make_async_copy(dst, dst, local_sem.at[i])
    kl, vl = long_v.at[0], long_v.at[1]
    ks, vs = cache_v.at[0], cache_v.at[1]
    slot_v, len_v = index_v.at[0], index_v.at[1]

    sent = []

    def stage(blocks, copies):
        k = len(sent)
        for src, dst, peer in copies:
            pltpu.make_async_remote_copy(
                src_ref=src, dst_ref=dst, send_sem=send_sem.at[k], recv_sem=recv_sem.at[k],
                device_id=peer, device_id_type=MESH,
            ).start()
        sent.append(pltpu.make_async_copy(blocks, blocks, send_sem.at[k]))
        return pltpu.make_async_copy(blocks, blocks, recv_sem.at[k])

    @pl.when(c == 1)
    def _():
        pl.semaphore_wait(barrier, nc * (nx - 1 + ny - 1) + 1)
        signal(ready_sem, partner)

    @pl.when(c == 0)
    def _():
        pl.semaphore_wait(ready_sem, 1)

    x1 = stage(hbuf.at[: nx - 1], [(hid_s, hbuf.at[t], p) for p in x_peer.values()])
    x1l = stage(hlbuf.at[: nx - 1], [(hid_l, hlbuf.at[t], p) for p in x_peer.values()])

    qz[:, 1 - c] = jnp.zeros((nz, ns, width), BF16)
    local["index"].wait()
    span = nz * nc * ns
    per = 128 // (nc * ns)
    ids = rows_of((nw * slot_dev, 128))
    ids = ids // (nc * slot_dev) * (nz * nc * slot_dev) + z * (nc * slot_dev) + lax.rem(ids, nc * slot_dev)
    for i in range(span // 128):
        row = slot_v[pl.ds(y * (span // 128) + i, 1), :]
        hit = jnp.where(ids == row, 1.0, 0.0)
        sel[:, i * 128 : (i + 1) * 128] = hit.astype(BF16)
        sel_t[i * per : (i + 1) * per] = (
            jnp.transpose(hit).astype(BF16).reshape(per, nc, ns, nw * slot_dev)
        )
    mine = rows_of((slot_dev, 128)) + s * slot_dev
    size = jnp.zeros((slot_dev, 128), F32)
    for i in range(total_rows):
        size += jnp.where(mine == slot_v[i : i + 1, :], len_v[i : i + 1, :].astype(F32), 0.0)
    size = jnp.sum(size, axis=1, keepdims=True)

    @pl.when(c == 0)
    def _():
        pl.semaphore_wait(barrier, nc * (nz - 1))
        signal(ready_sem, partner)

    @pl.when(c == 1)
    def _():
        pl.semaphore_wait(ready_sem, 1)

    for name in ("hs", "gain", "wq"):
        local[name].wait()
    x1.wait()
    gain = gain_v[...].reshape(1, width)
    hidden = jnp.concatenate([hbuf[i] for i in range(nx)], axis=1)
    q_short = head_unit(dot_t(hidden, wq[...]), gain).astype(BF16)
    qz[z, c] = q_short
    f1 = stage(qz.at[: nz - 1, c], [(qz.at[z, c], qz.at[z, c], p) for p in z_peer.values()])

    local["hl"].wait()
    x1l.wait()
    hidden_l = jnp.concatenate([hlbuf[i].astype(F32) for i in range(nx)], axis=1)
    hidden_l = jnp.concatenate([hidden_l, jnp.zeros((LROWS - long_count, depth), F32)], axis=0)
    q_long = head_unit(dot_t(hidden_l.astype(BF16), wq[...]), gain).astype(BF16)
    local["long"].wait()
    positions = kl.shape[0] * kl.shape[2]
    valid = lanes((LROWS, positions)) // kl.shape[2] == rows_of((LROWS, positions))
    num, den = attend(
        q_long.astype(F32) * math.sqrt(HEAD),
        side_by_side(kl, 0, long_count),
        side_by_side(vl, 0, long_count),
        valid,
    )
    l1s[:, :width] = num
    l1s[:, width - 64 :] = tail_of(l1s[:, width - 64 :], den)
    l1r[w] = l1s[...]
    l1 = stage(l1r.at[: nw - 1], [(l1s, l1r.at[w], p) for p in w_peer.values()])

    local["wkv"].wait()
    state = jnp.concatenate([hidden.astype(F32), hidden_l], axis=0)
    every = state.astype(BF16)
    query = jnp.concatenate([q_short.astype(F32), q_long.astype(F32)], axis=0)
    new_key = head_unit(dot_t(every, wkv[0]), gain).astype(BF16).astype(F32)
    new_value = dot_t(every, wkv[1]).astype(BF16).astype(F32)
    own = [jnp.exp(v * math.sqrt(HEAD)) for v in head_sums(query * new_key)]
    own_value = spread([v.astype(BF16).astype(F32) for v in own], new_value.shape) * new_value

    f1.wait()
    picked = dot(sel[...], qz[...].reshape(span, width))
    for u in range(nw):
        f2s[u] = fold(picked[u * slot_dev : (u + 1) * slot_dev])
    f2 = stage(f2r.at[: nw - 1], [(f2s.at[v], f2r.at[w], w_peer[d]) for d, v in w_at.items()])
    f2r[w] = f2s[w]

    l1.wait()
    l2s[...] = jnp.sum(l1r[...], axis=0)
    l2r[z] = l2s[...]
    l2 = stage(l2r.at[: nz - 1], [(l2s, l2r.at[z], p) for p in z_peer.values()])

    local["cache"].wait()
    f2.wait()
    q_slot = unfold(jnp.sum(f2r[...].astype(F32), axis=0), slot_dev) * math.sqrt(HEAD)
    half = slot_dev // 2
    r1 = [
        stage(
            r1r.at[: nw - 1, pl.ds(lo, half)],
            [(r1s.at[pl.ds(lo, half)], r1r.at[w, pl.ds(lo, half)], p) for p in w_peer.values()],
        )
        for lo in range(0, slot_dev, half)
        if attend_slots(q_slot, ks, vs, size, r1s, lo, lo + half) is None
    ]
    r1r[w] = r1s[...]

    local["rate"].wait()
    local["wo"].wait()
    rate = rate_v[...].reshape(1, depth)

    def attended(sums, lo, hi):
        own_part = [v[lo:hi] for v in own]
        under = [a + b for a, b in zip(columns_of(sums[:, width - 64 :], heads), own_part, strict=True)]
        return ((sums[:, :width] + own_value[lo:hi]) / spread(under, (hi - lo, width))).astype(BF16)

    def updated(proj, lo, hi):
        update = state[lo:hi] + rate * (row_unit(proj) - state[lo:hi])
        result = row_unit(update)
        return pltpu.roll(result, lax.rem(depth - t * width, depth), 1)[:, :width]

    l2.wait()
    x3s[...] = dot(attended(jnp.sum(l2r[...], axis=0), ns, ns + LROWS), wo[...])
    x3r[t] = x3s[...]
    x3 = stage(x3r.at[: nx - 1], [(x3s, x3r.at[t], p) for p in x_peer.values()])

    for part in r1:
        part.wait()
    back = dot(sel_t[:, c].reshape(nz * ns, nw * slot_dev), r1r[...].reshape(nw * slot_dev, width + 64))
    r2s[...] = back.astype(BF16).reshape(nz, ns, width + 64)
    r2 = stage(
        r2r.at[: nz - 1], [(r2s.at[lax.rem(z + d, nz)], r2r.at[z], p) for d, p in z_peer.items()]
    )
    r2r[z] = r2s[z]

    x3.wait()
    out_l[...] = updated(jnp.sum(x3r[...], axis=0), ns, ns + LROWS)[:long_count].astype(BF16)

    r2.wait()
    sums = jnp.sum(r2r[...].astype(F32), axis=0)
    ready = attended(sums, 0, ns)
    x2 = []
    for lo in range(0, depth, depth // 2):
        cols = pl.ds(lo, depth // 2)
        x2s[:, cols] = dot(ready, wo[:, cols]).astype(BF16)
        x2.append(
            stage(
                x2r.at[: nx - 1, :, cols],
                [(x2s.at[:, cols], x2r.at[t, :, cols], p) for p in x_peer.values()],
            )
        )
    x2r[t] = x2s[...]
    for part in x2:
        part.wait()
    out_s[...] = updated(jnp.sum(x2r[...].astype(F32), axis=0), 0, ns).astype(BF16)

    for part in sent:
        part.wait()


def hand_over(a_s, a_l, out_s, out_l, sem):
    copies = [
        pltpu.make_async_copy(a_s, out_s, sem.at[0]),
        pltpu.make_async_copy(a_l, out_l, sem.at[1]),
    ]
    for copy in copies:
        copy.start()
    for copy in copies:
        copy.wait()


def on_device(
    sizes,
    short_hidden, long_hidden, short_len, short_slot, w_query, w_key, w_value, w_out, qk_gain, step_rate,
    short_keys, short_values, long_keys, long_values,
):
    ny, nz, nc, nx = sizes
    nw = ny * nc
    ns, width = short_hidden.shape
    long_count = long_hidden.shape[0]
    depth = w_query.shape[0]
    slot_dev = short_keys.shape[0]
    wide = width + 64
    total = short_slot.shape[0]
    span = nz * nc * ns
    dma = pltpu.SemaphoreType.DMA
    args = (
        short_hidden, long_hidden, short_len.reshape(total // 128, 128), short_slot.reshape(total // 128, 128),
        w_query.T, w_key.T, w_value.T, w_out, qk_gain, step_rate,
        *(a.transpose(0, 2, 1) for a in (short_keys, short_values, long_keys, long_values)),
    )
    vmem = pltpu.VMEM
    scratch = [
        vmem((nx, ns, width), BF16), vmem((nx, long_count, width), BF16),
        vmem((2, total // 128, 128), jnp.int32), vmem((width, depth), BF16), vmem((2, width, depth), BF16),
        vmem((width, depth), BF16), vmem((width,), F32), vmem((depth,), F32),
        vmem((2, *args[10].shape), BF16), vmem((2, *args[12].shape), BF16),
        vmem((nw * slot_dev, span), BF16), vmem((nz, nc, ns, nw * slot_dev), BF16),
        vmem((nz, nc, ns, width), BF16),
        *(vmem((nw, slot_dev // 2 * (width // HEAD), 128), BF16) for _ in range(2)),
        vmem((slot_dev, wide), BF16), vmem((nw, slot_dev, wide), BF16),
        vmem((nz, ns, wide), BF16), vmem((nz, ns, wide), BF16), vmem((slot_dev, wide), F32),
        vmem((LROWS, wide), F32), vmem((nw, LROWS, wide), F32),
        vmem((LROWS, wide), F32), vmem((nz, LROWS, wide), F32),
        vmem((ns, depth), BF16), vmem((nx, ns, depth), BF16),
        vmem((LROWS, depth), F32), vmem((nx, LROWS, depth), F32),
        dma((10,)), dma((12,)), dma((12,)), pltpu.SemaphoreType.REGULAR,
    ]
    results = pl.pallas_call(
        functools.partial(kernel, sizes),
        out_shape=(vmem(short_hidden.shape, BF16), vmem(long_hidden.shape, BF16)),
        in_specs=[pl.BlockSpec(memory_space=pl.ANY)] * len(args),
        out_specs=(pl.BlockSpec(memory_space=vmem), pl.BlockSpec(memory_space=vmem)),
        scratch_shapes=scratch,
        compiler_params=pltpu.CompilerParams(collective_id=0, has_side_effects=True),
    )(*args)
    return pl.pallas_call(
        hand_over,
        out_shape=tuple(jax.ShapeDtypeStruct(a.shape, a.dtype) for a in results),
        in_specs=[pl.BlockSpec(memory_space=vmem)] * 2,
        out_specs=(pl.BlockSpec(memory_space=pl.ANY), pl.BlockSpec(memory_space=pl.ANY)),
        scratch_shapes=[dma((2,))],
    )(*(pltpu.with_memory_space_constraint(a, pltpu.VMEM) for a in results))


def solution(mesh):
    sizes = (*GRID[mesh.shape["seq"]], mesh.shape["tp"])
    return jax.shard_map(
        functools.partial(on_device, sizes),
        mesh=mesh,
        in_specs=(
            P("seq", "tp"),
            P(None, "tp"),
            P(),
            P(),
            P(None, "tp"),
            P(None, "tp"),
            P(None, "tp"),
            P("tp", None),
            P("tp"),
            P(),
            P("seq", None, "tp"),
            P("seq", None, "tp"),
            P(None, "seq", "tp"),
            P(None, "seq", "tp"),
        ),
        out_specs=(P("seq", "tp"), P(None, "tp")),
        check_vma=False,
    )
```
